32 devices in a mesh: dp: 4 (over x, core), seq: 8 (over z, y).
Axes of the slice: x: 2, y: 2, z: 4, core: 2. Of those that a mesh axis runs over, the one named last changes fastest.
Arguments:
- inputs: bfloat16 [4, 8192, 384], P('dp', 'seq'), may hold values from -6 to 6
- cotangent: bfloat16 [4, 8192, 384], P('dp', 'seq'), may hold values from -6 to 6
- first_dilated_kernel: bfloat16 [3, 384, 192], replicated, may hold values from -0.1875 to 0.1875
- first_pointwise_weight: bfloat16 [192, 384], replicated, may hold values from -0.4375 to 0.4375
- second_dilated_kernel: bfloat16 [3, 384, 192], replicated, may hold values from -0.1875 to 0.1875
- second_pointwise_weight: bfloat16 [192, 384], replicated, may hold values from -0.4375 to 0.4375
Outputs:
- input_gradient: bfloat16 [4, 8192, 384], P('dp', 'seq')
- conv_first_grad: float32 [3, 384, 192], P(None, 'dp')
- point_first_grad: float32 [192, 384], P(None, 'dp')
- conv_second_grad: float32 [3, 384, 192], P(None, 'dp')
- point_second_grad: float32 [192, 384], P(None, 'dp')
The draws below stay inside these ranges and needn't reach their ends.
All inputs are finite; a program needn't handle non-finite values.
Results may differ from the reference program's by a relative error of at most 0.0071.
Values may be sent and summed in bfloat16 or wider, within the bound.
No kernel may reach another device: no remote copies, remote signals or barrier semaphores. Data moves between devices by JAX's collectives and lax.ppermute only.
A program may use at most 64 MiB of HBM per device.

```python
import math
import jax
import jax.numpy as jnp
from jax import lax

C = 384
M = 192
DILATION_ONE = 2048
DILATION_TWO = 4096
SAMPLES = 4
SEQ_LEN = 8192


def raised(entries, key, source, target, parts, factor):
    def block_of(dim):
        return (jnp.arange(entries.shape[dim]) // (entries.shape[dim] // parts)).reshape((-1,) + (1,) * (entries.ndim - 1 - dim))

    first = jax.random.permutation(key, parts)[block_of(target)]
    far = (block_of(target) + parts // 2) % parts
    return jnp.where((block_of(source) == first) | (block_of(source) == far), factor * entries, entries)


def block_levels(stream_key, dims, shards, low, top_value):
    factor_of = 1.0
    for axis_at, parts in shards:
        draws = jax.random.uniform(jax.random.fold_in(jax.random.fold_in(stream_key, 6), axis_at), (parts,), jnp.float32, low / len(shards), top_value / len(shards))
        factor_of = factor_of * jnp.repeat(jnp.exp(draws), dims[axis_at] // parts).reshape((-1,) + (1,) * (len(dims) - 1 - axis_at))
    return factor_of


def centred(rng, shape, deviation, limit, split=(), kind=jnp.bfloat16):
    drawn = jax.random.normal(rng, shape, jnp.float32) * deviation
    if len(split) > 0:
        drawn = block_levels(rng, shape, split, -0.22, 0.18) * drawn
    return jnp.clip(drawn, min=-limit, max=limit).astype(kind)


def noise_with(rng, shape, spread, most, pieces, heavy, kind=jnp.bfloat16):
    values = spread * jax.random.normal(rng, shape, jnp.float32)
    if pieces:
        values = values * block_levels(rng, shape, pieces, -0.22, 0.18)
    return jnp.clip(raised(values, jax.random.fold_in(rng, 3), *heavy), -most, most).astype(kind)


def setup_inputs(seed: int = 0) -> dict:
    keys = jax.random.split(jax.random.key(seed), 7)
    return {
        "inputs": centred(keys[0], (SAMPLES, SEQ_LEN, C), 1.0, 6.0, ((0, 4), (1, 8))),
        "cotangent": noise_with(keys[1], (SAMPLES, SEQ_LEN, C), 1.0, 6.0, ((0, 4), (1, 8)), (1, 2, 8, 2.0)),
        "first_dilated_kernel": centred(keys[2], (3, C, M), (3 * C) ** -0.5, 0.1875),
        "first_pointwise_weight": centred(keys[3], (M, C), M ** -0.5, 0.4375),
        "second_dilated_kernel": centred(keys[4], (3, C, M), (3 * C) ** -0.5, 0.1875),
        "second_pointwise_weight": centred(keys[5], (M, C), M ** -0.5, 0.4375),
    }


def gelu_parts(values):
    coeff = math.sqrt(2.0 / math.pi)
    inner = coeff * (values + 0.044715 * values * values * values)
    tanh_val = jnp.tanh(inner)
    value = 0.5 * values * (1.0 + tanh_val)
    slope = 0.5 * (1.0 + tanh_val) + 0.5 * values * (1.0 - tanh_val * tanh_val) * coeff * (1.0 + 3.0 * 0.044715 * values * values)
    return (value, slope)

def rows_after(rows, dilation):
    zeros = jnp.zeros((dilation, rows.shape[1]), rows.dtype)
    return jnp.concatenate([rows[dilation:], zeros], axis=0)

def rows_before(rows, dilation):
    zeros = jnp.zeros((dilation, rows.shape[1]), rows.dtype)
    return jnp.concatenate([zeros, rows[:-dilation]], axis=0)

def matmul(left, right):
    return jnp.dot(left, right, preferred_element_type=jnp.float32)

def residual_block_forward(state, kernel, pointwise, dilation):
    act = gelu_parts(state.astype(jnp.float32))[0].astype(jnp.bfloat16)
    pre = matmul(rows_before(act, dilation), kernel[0]) + matmul(act, kernel[1]) + matmul(rows_after(act, dilation), kernel[2])
    mid_val, pre_slope = gelu_parts(pre)
    mid = mid_val.astype(jnp.bfloat16)
    output = (state.astype(jnp.float32) + matmul(mid, pointwise)).astype(jnp.bfloat16)
    return (output, act, pre_slope, mid)

def residual_block_backward(state, upstream, kernel, pointwise, dilation, act, pre_slope, mid):
    mid_grad = matmul(upstream, pointwise.T)
    pre_grad = (mid_grad * pre_slope).astype(jnp.bfloat16)
    grad_after = rows_after(pre_grad, dilation)
    grad_before = rows_before(pre_grad, dilation)
    point_sum = matmul(mid.T, upstream)
    conv_sum = jnp.stack([matmul(act.T, grad_after), matmul(act.T, pre_grad), matmul(act.T, grad_before)])
    act_grad = matmul(grad_after, kernel[0].T) + matmul(pre_grad, kernel[1].T) + matmul(grad_before, kernel[2].T)
    state_slope = gelu_parts(state.astype(jnp.float32))[1]
    state_grad = (upstream.astype(jnp.float32) + act_grad * state_slope).astype(jnp.bfloat16)
    return (state_grad, conv_sum, point_sum)

def reference(inputs, cotangent, first_dilated_kernel, first_pointwise_weight, second_dilated_kernel, second_pointwise_weight):

    def one_sample(pair):
        sample_input, sample_upstream_gradient = pair
        hidden_block_state, first_block_activation, first_gelu_derivative, first_middle_value = residual_block_forward(sample_input, first_dilated_kernel, first_pointwise_weight, DILATION_ONE)
        ignored_placeholder, second_block_activation, second_gelu_derivative, second_middle_value = residual_block_forward(hidden_block_state, second_dilated_kernel, second_pointwise_weight, DILATION_TWO)
        second_block_gradient, second_kernel_value, second_pointwise_value = residual_block_backward(hidden_block_state, sample_upstream_gradient, second_dilated_kernel, second_pointwise_weight, DILATION_TWO, second_block_activation, second_gelu_derivative, second_middle_value)
        input_gradient, first_kernel_value, first_pointwise_value = residual_block_backward(sample_input, second_block_gradient, first_dilated_kernel, first_pointwise_weight, DILATION_ONE, first_block_activation, first_gelu_derivative, first_middle_value)
        return (input_gradient, first_kernel_value, first_pointwise_value, second_kernel_value, second_pointwise_value)
    input_gradient, first_kernel_value, first_pointwise_value, second_kernel_value, second_pointwise_value = lax.map(one_sample, (inputs, cotangent))
    scale = 1.0 / math.sqrt(SAMPLES * SEQ_LEN)
    return (input_gradient, lax.optimization_barrier(jnp.sum(first_kernel_value, axis=0)) * scale, lax.optimization_barrier(jnp.sum(first_pointwise_value, axis=0)) * scale, lax.optimization_barrier(jnp.sum(second_kernel_value, axis=0)) * scale, lax.optimization_barrier(jnp.sum(second_pointwise_value, axis=0)) * scale)
```

```python
import functools
import math

import jax
import jax.numpy as jnp
from jax import lax
from jax.experimental import pallas as pl
from jax.experimental.pallas import tpu as pltpu
from jax.sharding import PartitionSpec as P

DILATION_ONE = 2048
DILATION_TWO = 4096
TILE = 256
CHUNK = 32
MAX_PERMUTES = 8
BF16 = jnp.bfloat16
F32 = jnp.float32


def gelu_parts(values):
    coeff = math.sqrt(2.0 / math.pi)
    square = values * values
    tanh_val = jnp.tanh(values * (coeff + (coeff * 0.044715) * square))
    half = 0.5 + 0.5 * tanh_val
    slope = half + half * (1.0 - tanh_val) * (values * (coeff + (3.0 * coeff * 0.044715) * square))
    return values * half, slope


def dot(left, right):
    return jnp.dot(left, right, preferred_element_type=F32)


def dot_nt(left, right):
    return lax.dot_general(left, right, (((1,), (1,)), ((), ())), preferred_element_type=F32)


def position(hop):
    return lax.axis_index("seq") // hop


def place(parts, rows_ref, hop):
    if len(parts) == 1:
        rows_ref[...] = parts[0][...]
        return
    count = len(parts)
    size = rows_ref.shape[0] // count
    me = position(hop)
    for k, part in enumerate(parts):
        at = lax.rem(me + (count - k), count)
        rows_ref[pl.ds(pl.multiple_of(at * size, size), size), :] = part[...]


def hand_out(rows_ref, parts, hop):
    if len(parts) == 1:
        parts[0][...] = rows_ref[...]
        return
    count = len(parts)
    size = rows_ref.shape[0] // count
    me = position(hop)
    for k, part in enumerate(parts):
        at = lax.rem(me + k, count)
        part[...] = rows_ref[pl.ds(pl.multiple_of(at * size, size), size), :]


def tap_sum(padded_ref, shift, start, weight_of, mm):
    total = mm(padded_ref[pl.ds(start + shift, TILE), :], weight_of(1))
    rows = padded_ref.shape[0] - 2 * shift
    if start + TILE > shift:
        total = total + mm(padded_ref[pl.ds(start, TILE), :], weight_of(0))
    if start < rows - shift:
        total = total + mm(padded_ref[pl.ds(start + 2 * shift, TILE), :], weight_of(2))
    return total


def clear_edges(padded_ref, shift):
    rows = padded_ref.shape[0]
    zeros = jnp.zeros((shift, padded_ref.shape[1]), padded_ref.dtype)
    padded_ref[pl.ds(0, shift), :] = zeros
    padded_ref[pl.ds(rows - shift, shift), :] = zeros


def forward_kernel(shifts, hop, count, *refs):
    parts = refs[:count]
    k1t, p1, k2t = refs[count : count + 3]
    outs = refs[count + 3 : count + 11]
    act1_t, mid1_t, s_x, s_p1, act2_t, mid2_t, s_h, s_p2 = outs
    x_rows, pad1, pad2, wide, narrow = refs[count + 11 :]
    rows = x_rows.shape[0]
    place(parts, x_rows, hop)

    def activate(source, source_start, pad, shift, start, slope_ref):
        def step(i, carry):
            at = pl.multiple_of(i * CHUNK, CHUNK)
            value, slope = gelu_parts(
                source[pl.ds(source_start + at, CHUNK), :].astype(F32)
            )
            pad[pl.ds(start + shift + at, CHUNK), :] = value.astype(BF16)
            slope_ref[pl.ds(start + at, CHUNK), :] = slope
            return carry

        lax.fori_loop(0, TILE // CHUNK, step, 0, unroll=2)

    def narrow_gelu(start, slope_ref):
        def step(i, carry):
            at = pl.multiple_of(i * CHUNK, CHUNK)
            value, slope = gelu_parts(narrow[pl.ds(at, CHUNK), :])
            narrow[pl.ds(at, CHUNK), :] = value
            slope_ref[pl.ds(start + at, CHUNK), :] = slope
            return carry

        lax.fori_loop(0, TILE // CHUNK, step, 0, unroll=2)

    clear_edges(pad1, shifts[0])
    clear_edges(pad2, shifts[1])
    for start in range(0, rows, TILE):
        activate(x_rows, start, pad1, shifts[0], start, s_x)
        act1_t[:, pl.ds(start, TILE)] = pad1[pl.ds(start + shifts[0], TILE), :].T
    for start in range(0, rows, TILE):
        narrow[...] = tap_sum(pad1, shifts[0], start, lambda k: k1t[k], dot_nt)
        narrow_gelu(start, s_p1)
        mid = narrow[...].astype(BF16)
        mid1_t[:, pl.ds(start, TILE)] = mid.T
        wide[...] = (x_rows[pl.ds(start, TILE), :].astype(F32) + dot(mid, p1[...])).astype(BF16)
        activate(wide, 0, pad2, shifts[1], start, s_h)
        act2_t[:, pl.ds(start, TILE)] = pad2[pl.ds(start + shifts[1], TILE), :].T
    for start in range(0, rows, TILE):
        narrow[...] = tap_sum(pad2, shifts[1], start, lambda k: k2t[k], dot_nt)
        narrow_gelu(start, s_p2)
        mid2_t[:, pl.ds(start, TILE)] = narrow[...].astype(BF16).T


def backward_kernel(shift, hop, n_in, n_out, *refs):
    parts = refs[:n_in]
    act_t, mid_t, s_state, s_pre, kt, point = refs[n_in : n_in + 6]
    outs = refs[n_in + 6 : n_in + 6 + n_out]
    keep, send = refs[n_in + 6 + n_out : n_in + 8 + n_out]
    g_rows, pad, grads, x_rows = refs[n_in + 8 + n_out :]
    rows = g_rows.shape[0]
    place(parts, g_rows, hop)
    clear_edges(pad, shift)
    for start in range(0, rows, TILE):
        mid_grad = dot_nt(g_rows[pl.ds(start, TILE), :], point[...])
        pad[pl.ds(start + shift, TILE), :] = (mid_grad * s_pre[pl.ds(start, TILE), :]).astype(BF16)
    for start in range(0, rows, TILE):
        act_grad = tap_sum(pad, shift, start, lambda k: kt[2 - k], dot)
        x_rows[pl.ds(start, TILE), :] = (
            g_rows[pl.ds(start, TILE), :].astype(F32) + act_grad * s_state[pl.ds(start, TILE), :]
        ).astype(BF16)
    hand_out(x_rows, outs, hop)
    act = act_t[...]
    grads[...] = jnp.concatenate(
        [
            dot(act, pad[pl.ds(2 * shift, rows), :]),
            dot(act, pad[pl.ds(shift, rows), :]),
            dot(act, pad[pl.ds(0, rows), :]),
            dot(mid_t[...], g_rows[...]).T,
        ],
        axis=1,
    )
    size = keep.shape[1]
    core = lax.rem(lax.axis_index("dp"), 2)
    for half in range(2):
        for target, parity in ((keep, core), (send, 1 - core)):
            at = pl.multiple_of((2 * half + parity) * size, size)
            target[half] = grads[pl.ds(at, size), :].astype(BF16)


def split_kernel(keep, received, *pieces):
    x_at = lax.axis_index("dp") // 2
    y_at = lax.rem(lax.axis_index("seq"), 2)
    size = pieces[0].shape[0]
    for k, piece in enumerate(pieces):
        x_to = lax.rem(x_at + k // 2, 2)
        rows = pl.ds(pl.multiple_of(lax.rem(y_at + k, 2) * size, size), size)
        piece[...] = (keep[x_to, rows, :].astype(F32) + received[x_to, rows, :].astype(F32)).astype(BF16)


def sum_kernel(*refs):
    total = refs[0][...].astype(F32)
    for ref in refs[1:-1]:
        total = total + ref[...].astype(F32)
    refs[-1][...] = total.astype(BF16)


def ordered_sum_kernel(hop, *refs):
    *parts, out, held = refs
    count = len(parts)
    me = position(hop)
    for k, part in enumerate(parts):
        held[lax.rem(me + (count - k), count)] = part[...]
    total = held[0].astype(F32)
    for k in range(1, count):
        total = total + held[k].astype(F32)
    out[...] = total.astype(BF16)


def finish_kernel(scale, own, other, conv, point, rows):
    y_at = lax.rem(lax.axis_index("seq"), 2)
    size = own.shape[0]
    rows[pl.ds(pl.multiple_of(y_at * size, size), size), :] = own[...].astype(F32) * scale
    rows[pl.ds(pl.multiple_of((1 - y_at) * size, size), size), :] = other[...].astype(F32) * scale
    width = conv.shape[2]
    whole = rows[...]
    for k in range(3):
        conv[k] = whole[:, k * width : (k + 1) * width]
    point[...] = whole[:, 3 * width :].T


def call(kernel, out_shapes, scratch, *args):
    vmem = pl.BlockSpec(memory_space=pltpu.VMEM)
    return pl.pallas_call(
        kernel,
        out_shape=[jax.ShapeDtypeStruct(s, d) for s, d in out_shapes],
        in_specs=[vmem] * len(args),
        out_specs=[vmem] * len(out_shapes),
        scratch_shapes=[pltpu.VMEM(s, d) for s, d in scratch],
        compiler_params=pltpu.CompilerParams(vmem_limit_bytes=48 << 20),
    )(*args)


def send_ahead(block, hop, k):
    size = lax.axis_size("seq")
    count = size // hop
    route = [(i, ((i // hop + k) % count) * hop + i % hop) for i in range(size)]
    return lax.ppermute(block, "seq", route)


def mirrored(block, dp_bits, seq_bits):
    n_dp, n_seq = lax.axis_size("dp"), lax.axis_size("seq")
    route = [
        (i * n_seq + j, (i ^ dp_bits) * n_seq + (j ^ seq_bits))
        for i in range(n_dp)
        for j in range(n_seq)
    ]
    return lax.ppermute(block, ("dp", "seq"), route)


def column_groups(hop):
    size = lax.axis_size("seq")
    return [list(range(first, size, hop)) for first in range(hop)]


def exchange_all(block, hop):
    count = lax.axis_size("seq") // hop
    cut = block.reshape(count, -1, block.shape[-1])
    swapped = lax.all_to_all(
        cut, "seq", 0, 0, axis_index_groups=column_groups(hop), tiled=True
    )
    return swapped.reshape(block.shape)


def to_columns(block, hop):
    count = lax.axis_size("seq") // hop
    if count > MAX_PERMUTES:
        return [exchange_all(block, hop)]
    size = block.shape[0] // count
    me = position(hop)
    pieces = [
        lax.dynamic_slice_in_dim(block, ((me + k) % count) * size, size, 0) for k in range(count)
    ]
    return [pieces[0]] + [send_ahead(pieces[k], hop, k) for k in range(1, count)]


def from_columns(parts, hop):
    if len(parts) == 1:
        return [exchange_all(parts[0], hop)]
    return [parts[0]] + [send_ahead(parts[k], hop, k) for k in range(1, len(parts))]


def collect_kernel(hop, *refs):
    place(refs[:-1], refs[-1], hop)


def reduce_weights(keep, send, hop, scale):
    half, rows, lanes = keep.shape
    width = lanes // 4
    received = mirrored(send, 1, 0)
    piece = ((rows // 2, lanes), BF16)
    pieces = call(split_kernel, [piece] * 4, [], keep, received)
    arrived = [pieces[0]] + [
        mirrored(pieces[k], 2 * (k // 2), k % 2) for k in range(1, 4)
    ]
    (plane,) = call(sum_kernel, [piece], [], *arrived)
    count = lax.axis_size("seq") // hop
    if count > MAX_PERMUTES:
        own = lax.psum(plane.astype(F32), "seq", axis_index_groups=column_groups(hop)).astype(BF16)
    else:
        column = [plane] + [send_ahead(plane, hop, k) for k in range(1, count)]
        (own,) = call(
            functools.partial(ordered_sum_kernel, hop),
            [piece],
            [((count, rows // 2, lanes), BF16)],
            *column,
        )
    other = mirrored(own, 0, 1)
    return call(
        functools.partial(finish_kernel, scale),
        [((3, rows, width), F32), ((width, rows), F32)],
        [((rows, lanes), F32)],
        own,
        other,
    )


def shards(
    inputs,
    cotangent,
    first_dilated_kernel,
    first_pointwise_weight,
    second_dilated_kernel,
    second_pointwise_weight,
):
    samples, rows, channels = inputs.shape
    width = first_pointwise_weight.shape[0]
    hop = DILATION_ONE // rows
    count = lax.axis_size("seq") // hop
    size = rows // count
    shifts = (size, size * (DILATION_TWO // DILATION_ONE))
    total_rows = samples * lax.axis_size("dp") * rows * lax.axis_size("seq")
    scale = 1.0 / math.sqrt(total_rows)
    k1t = jnp.swapaxes(first_dilated_kernel, 1, 2)
    k2t = jnp.swapaxes(second_dilated_kernel, 1, 2)

    x_parts = to_columns(inputs.reshape(rows, channels), hop)
    g_parts = to_columns(cotangent.reshape(rows, channels), hop)
    state = [
        ((channels, rows), BF16),
        ((width, rows), BF16),
        ((rows, channels), F32),
        ((rows, width), F32),
    ]
    saved = call(
        functools.partial(forward_kernel, shifts, hop, len(x_parts)),
        state * 2,
        [
            ((rows, channels), BF16),
            ((rows + 2 * shifts[0], channels), BF16),
            ((rows + 2 * shifts[1], channels), BF16),
            ((TILE, channels), BF16),
            ((TILE, width), F32),
        ],
        *x_parts,
        k1t,
        first_pointwise_weight,
        k2t,
    )
    part_shape = (x_parts[0].shape, BF16)
    whole_shape = ((rows, channels), BF16)

    def backward(g_in, saved, shift, kt, point, out_shapes):
        act_t, mid_t, s_state, s_pre = saved
        quarter = ((2, channels // 4, 4 * width), BF16)
        *outs, keep, send = call(
            functools.partial(backward_kernel, shift, hop, len(g_in), len(out_shapes)),
            out_shapes + [quarter, quarter],
            [
                whole_shape,
                ((rows + 2 * shift, width), BF16),
                ((channels, 4 * width), F32),
                whole_shape,
            ],
            *g_in,
            act_t,
            mid_t,
            s_state,
            s_pre,
            kt,
            point,
        )
        return outs, keep, send

    hidden_grad, keep2, send2 = backward(
        g_parts, saved[4:], shifts[1], k2t, second_pointwise_weight, [whole_shape]
    )
    conv2, point2 = reduce_weights(keep2, send2, hop, scale)
    x_grads, keep1, send1 = backward(
        hidden_grad, saved[:4], shifts[0], k1t, first_pointwise_weight, [part_shape] * len(x_parts)
    )
    conv1, point1 = reduce_weights(keep1, send1, hop, scale)
    back = from_columns(x_grads, hop)
    (input_grad,) = call(functools.partial(collect_kernel, hop), [whole_shape], [], *back)
    return input_grad.reshape(inputs.shape), conv1, point1, conv2, point2


def solution(mesh):
    return jax.shard_map(
        shards,
        mesh=mesh,
        in_specs=(P("dp", "seq", None), P("dp", "seq", None), P(), P(), P(), P()),
        out_specs=(
            P("dp", "seq", None),
            P(None, "dp", None),
            P(None, "dp"),
            P(None, "dp", None),
            P(None, "dp"),
        ),
        check_vma=False,
    )
```

```python
import functools
import math

import jax
import jax.numpy as jnp
from jax import lax
from jax.experimental import pallas as pl
from jax.experimental.pallas import tpu as pltpu
from jax.sharding import PartitionSpec as P

DILATION_ONE = 2048
DILATION_TWO = 4096
TILE = 256
CHUNK = 32
MAX_PERMUTES = 8
MERGED = True
AFTER = ((),(),(),1,)
BF16 = jnp.bfloat16
F32 = jnp.float32
VMEM = pl.BlockSpec(memory_space=pltpu.VMEM)
ANY = pl.BlockSpec(memory_space=pl.ANY)


def gelu_parts(values):
    coeff = math.sqrt(2.0 / math.pi)
    square = values * values
    tanh_val = jnp.tanh(values * (coeff + (coeff * 0.044715) * square))
    half = 0.5 + 0.5 * tanh_val
    slope = half + half * (1.0 - tanh_val) * (values * (coeff + (3.0 * coeff * 0.044715) * square))
    return values * half, slope


def dot(left, right):
    return jnp.dot(left, right, preferred_element_type=F32)


def dot_nt(left, right):
    return lax.dot_general(left, right, (((1,), (1,)), ((), ())), preferred_element_type=F32)


def position(hop):
    return lax.axis_index("seq") // hop


def behind(me, k, count):
    return lax.rem(me + (count - k), count)


def ahead(me, k, count):
    return lax.rem(me + k, count)


def call(kernel, out_shapes, scratch, args, after=(), mib=8):
    n_args, n_after = len(args), len(after)

    def body(*refs):
        kernel(*refs[:n_args], *refs[n_args + n_after :])

    return pl.pallas_call(
        body,
        out_shape=[jax.ShapeDtypeStruct(s, d) for s, d in out_shapes],
        in_specs=[VMEM] * n_args + [ANY] * n_after,
        out_specs=[VMEM] * len(out_shapes),
        scratch_shapes=[pltpu.VMEM(s, d) for s, d in scratch],
        compiler_params=pltpu.CompilerParams(vmem_limit_bytes=mib << 20),
    )(*args, *after)


def cut_kernel(hop, halves, block, *pieces):
    count = len(pieces) // halves
    step = pieces[0].shape[0]
    me = position(hop)
    for i, piece in enumerate(pieces):
        at = ahead(me, i % count, count) * (step * halves) + i // count * step
        piece[...] = block[pl.ds(pl.multiple_of(at, step), step), :]


def place(parts, rows_ref, hop, half=0):
    if len(parts) == 1:
        rows_ref[...] = parts[0][...]
        return
    count = len(parts)
    size = rows_ref.shape[0] // count
    me = position(hop)
    for k, part in enumerate(parts):
        at = pl.multiple_of(behind(me, k, count) * size, size)
        rows_ref[pl.ds(at, size), :] = part[pl.ds(half * size, size), :]


def hand_out(rows_ref, parts, hop):
    if len(parts) == 1:
        parts[0][...] = rows_ref[...]
        return
    count = len(parts)
    size = rows_ref.shape[0] // count
    me = position(hop)
    for k, part in enumerate(parts):
        at = pl.multiple_of(ahead(me, k, count) * size, size)
        part[...] = rows_ref[pl.ds(at, size), :]


def tap_sum(padded_ref, shift, start, tile, weight_of, mm):
    total = mm(padded_ref[pl.ds(start + shift, tile), :], weight_of(1))
    rows = padded_ref.shape[0] - 2 * shift
    if start + tile > shift:
        total = total + mm(padded_ref[pl.ds(start, tile), :], weight_of(0))
    if start < rows - shift:
        total = total + mm(padded_ref[pl.ds(start + 2 * shift, tile), :], weight_of(2))
    return total


def clear_edges(padded_ref, shift):
    rows = padded_ref.shape[0]
    zeros = jnp.zeros((shift, padded_ref.shape[1]), padded_ref.dtype)
    padded_ref[pl.ds(0, shift), :] = zeros
    padded_ref[pl.ds(rows - shift, shift), :] = zeros


def forward_kernel(shifts, hop, count, halves, *refs):
    parts = refs[:count]
    weights = refs[count : count + 3]
    outs = refs[count + 3 : count + 11]
    scratch = refs[count + 11 :]
    for half in range(halves):
        place(parts, scratch[0], hop, half)
        forward_half(shifts, weights, [out.at[half] for out in outs], scratch)


def forward_half(shifts, weights, outs, scratch):
    k1t, p1, k2t = weights
    act1_t, mid1_t, s_x, s_p1, act2_t, mid2_t, s_h, s_p2 = outs
    x_rows, pad1, pad2, wide, narrow = scratch
    rows = x_rows.shape[0]

    def activate(source, source_start, pad, shift, start, slope_ref):
        def step(i, carry):
            at = pl.multiple_of(i * CHUNK, CHUNK)
            value, slope = gelu_parts(source[pl.ds(source_start + at, CHUNK), :].astype(F32))
            pad[pl.ds(start + shift + at, CHUNK), :] = value.astype(BF16)
            slope_ref[pl.ds(start + at, CHUNK), :] = slope.astype(BF16)
            return carry

        lax.fori_loop(0, TILE // CHUNK, step, 0, unroll=2)

    def narrow_gelu(start, slope_ref):
        def step(i, carry):
            at = pl.multiple_of(i * CHUNK, CHUNK)
            value, slope = gelu_parts(narrow[pl.ds(at, CHUNK), :])
            narrow[pl.ds(at, CHUNK), :] = value
            slope_ref[pl.ds(start + at, CHUNK), :] = slope.astype(BF16)
            return carry

        lax.fori_loop(0, TILE // CHUNK, step, 0, unroll=2)

    clear_edges(pad1, shifts[0])
    clear_edges(pad2, shifts[1])
    for start in range(0, rows, TILE):
        activate(x_rows, start, pad1, shifts[0], start, s_x)
        act1_t[:, pl.ds(start, TILE)] = pad1[pl.ds(start + shifts[0], TILE), :].T
    for start in range(0, rows, TILE):
        narrow[...] = tap_sum(pad1, shifts[0], start, TILE, lambda k: k1t[k], dot_nt)
        narrow_gelu(start, s_p1)
        mid = narrow[...].astype(BF16)
        mid1_t[:, pl.ds(start, TILE)] = mid.T
        wide[...] = (x_rows[pl.ds(start, TILE), :].astype(F32) + dot(mid, p1[...])).astype(BF16)
        activate(wide, 0, pad2, shifts[1], start, s_h)
        act2_t[:, pl.ds(start, TILE)] = pad2[pl.ds(start + shifts[1], TILE), :].T
    for start in range(0, rows, TILE):
        narrow[...] = tap_sum(pad2, shifts[1], start, TILE, lambda k: k2t[k], dot_nt)
        narrow_gelu(start, s_p2)
        mid2_t[:, pl.ds(start, TILE)] = narrow[...].astype(BF16).T


def backward_kernel(shift, hop, half, n_in, n_out, first, last, *refs):
    parts = refs[:n_in]
    act_t, mid_t, s_state, s_pre = (ref.at[half] for ref in refs[n_in : n_in + 4])
    kt, point = refs[n_in + 4 : n_in + 6]
    at = n_in + 6
    if not first:
        so_far = refs[at]
        at += 1
    outs = refs[at : at + n_out]
    at += n_out
    if last:
        keep, send = refs[at : at + 2]
        at += 2
        g_rows, pad, x_rows, grads = refs[at:]
    else:
        grads = refs[at]
        g_rows, pad, x_rows = refs[at + 1 :]
    rows = g_rows.shape[0]
    place(parts, g_rows, hop)
    clear_edges(pad, shift)
    for start in range(0, rows, TILE):
        mid_grad = dot_nt(g_rows[pl.ds(start, TILE), :], point[...])
        pad[pl.ds(start + shift, TILE), :] = (
            mid_grad * s_pre[pl.ds(start, TILE), :].astype(F32)
        ).astype(BF16)
    for start in range(0, rows, TILE):
        act_grad = tap_sum(pad, shift, start, TILE, lambda k: kt[2 - k], dot)
        x_rows[pl.ds(start, TILE), :] = (
            g_rows[pl.ds(start, TILE), :].astype(F32)
            + act_grad * s_state[pl.ds(start, TILE), :].astype(F32)
        ).astype(BF16)
    hand_out(x_rows, outs, hop)
    act = act_t[...]
    total = jnp.concatenate(
        [
            dot(act, pad[pl.ds(2 * shift, rows), :]),
            dot(act, pad[pl.ds(shift, rows), :]),
            dot(act, pad[pl.ds(0, rows), :]),
            dot(mid_t[...], g_rows[...]).T,
        ],
        axis=1,
    )
    if not first:
        total = total + so_far[...]
    grads[...] = total
    if last:
        size = keep.shape[1]
        core = lax.rem(lax.axis_index("dp"), 2)
        for x_to in range(2):
            for target, parity in ((keep, core), (send, 1 - core)):
                rows_at = pl.multiple_of((2 * x_to + parity) * size, size)
                target[x_to] = grads[pl.ds(rows_at, size), :].astype(BF16)


def split_kernel(*refs):
    pieces = refs[-4:]
    pairs = list(zip(refs[0:-4:2], refs[1:-4:2]))
    x_at = lax.axis_index("dp") // 2
    y_at = lax.rem(lax.axis_index("seq"), 2)
    size = pieces[0].shape[1]
    for k, piece in enumerate(pieces):
        x_to = lax.rem(x_at + k // 2, 2)
        rows = pl.ds(pl.multiple_of(lax.rem(y_at + k, 2) * size, size), size)
        for i, (keep, received) in enumerate(pairs):
            total = keep[x_to, rows, :].astype(F32) + received[x_to, rows, :].astype(F32)
            piece[i] = total.astype(piece.dtype)


def sum_of(refs):
    total = refs[0][...].astype(F32)
    for ref in refs[1:]:
        total = total + ref[...].astype(F32)
    return total


def sum_kernel(*refs):
    refs[-1][...] = sum_of(refs[:-1]).astype(refs[-1].dtype)


def halve_kernel(hop, *refs):
    *parts, keep, send, total = refs
    total[...] = sum_of(parts)
    size = keep.shape[1]
    mine = lax.rem(position(hop), 2)
    for target, half in ((keep, mine), (send, 1 - mine)):
        target[...] = total[:, pl.ds(pl.multiple_of(half * size, size), size), :].astype(target.dtype)


def finish_kernel(scale, hop, n_blocks, *refs):
    parts, outs, rows = refs[: -2 * n_blocks - 1], refs[-2 * n_blocks - 1 : -1], refs[-1]
    z_at = lax.rem(position(hop), 2)
    y_at = lax.rem(lax.axis_index("seq"), 2)
    size = parts[0].shape[1]
    per_y = rows.shape[1] // 2
    for k, part in enumerate(parts):
        at = lax.rem(y_at + k, 2) * per_y
        if len(parts) > 2:
            at = at + lax.rem(z_at + k // 2, 2) * size
        rows[:, pl.ds(pl.multiple_of(at, size), size), :] = part[...].astype(F32) * scale
    for i in range(n_blocks):
        conv, point = outs[2 * i : 2 * i + 2]
        width = conv.shape[2]
        whole = rows[i]
        for k in range(3):
            conv[k] = whole[:, k * width : (k + 1) * width]
        point[...] = whole[:, 3 * width :].T


def collect_kernel(hop, halves, *refs):
    *parts, out = refs
    count = len(parts) // halves
    size = out.shape[0] // count
    step = size // halves
    me = position(hop)
    for h in range(halves):
        for k in range(count):
            at = pl.multiple_of(behind(me, k, count) * size + h * step, step)
            out[pl.ds(at, step), :] = parts[h * count + k][...]


def send_ahead(block, hop, k):
    size = lax.axis_size("seq")
    count = size // hop
    route = [(i, ((i // hop + k) % count) * hop + i % hop) for i in range(size)]
    return lax.ppermute(block, "seq", route)


def mirrored(block, dp_bits, seq_bits):
    n_dp, n_seq = lax.axis_size("dp"), lax.axis_size("seq")
    route = [
        (i * n_seq + j, (i ^ dp_bits) * n_seq + (j ^ seq_bits))
        for i in range(n_dp)
        for j in range(n_seq)
    ]
    return lax.ppermute(block, ("dp", "seq"), route)


def column_groups(hop):
    size = lax.axis_size("seq")
    return [list(range(first, size, hop)) for first in range(hop)]


def exchange_all(block, hop):
    count = lax.axis_size("seq") // hop
    cut = block.reshape(count, -1, block.shape[-1])
    swapped = lax.all_to_all(cut, "seq", 0, 0, axis_index_groups=column_groups(hop), tiled=True)
    return swapped.reshape(block.shape)


def to_columns(block, hop, halves, after=()):
    count = lax.axis_size("seq") // hop
    rows, channels = block.shape
    if count > MAX_PERMUTES:
        return [[exchange_all(block, hop)]]
    n_pieces = count * halves
    pieces = call(
        functools.partial(cut_kernel, hop, halves),
        [((rows // n_pieces, channels), BF16)] * n_pieces,
        [],
        [block],
        after,
        mib=2,
    )
    return [forward_pieces(pieces[h * count : (h + 1) * count], hop) for h in range(halves)]


def forward_pieces(pieces, hop):
    return [pieces[0]] + [send_ahead(pieces[k], hop, k) for k in range(1, len(pieces))]


def reduce_weights(blocks, hop, scale, after=()):
    n_blocks = len(blocks)
    _, rows, lanes = blocks[0][0].shape
    width = lanes // 4
    count = lax.axis_size("seq") // hop
    pairs = []
    for keep, send in blocks:
        pairs += [keep, mirrored(send, 1, 0)]
    half = (n_blocks, rows // 2, lanes)
    fourth = (n_blocks, rows // 4, lanes)
    pieces = call(split_kernel, [(half, F32)] + [(half, BF16)] * 3, [], pairs, AFTER[0] and after)
    arrived = [pieces[0]] + [mirrored(pieces[k], 2 * (k // 2), k % 2) for k in range(1, 4)]
    if count == 4:
        keep, send = call(
            functools.partial(halve_kernel, hop), [(fourth, F32), (fourth, BF16)], [(half, F32)], arrived, AFTER[1] and after
        )
        (pair,) = call(sum_kernel, [(fourth, BF16)], [], [keep, mirrored(send, 0, hop)], AFTER[2] and after)
        (own,) = call(sum_kernel, [(fourth, BF16)], [], [pair, mirrored(pair, 0, 2 * hop)], AFTER[3] and after)
        parts = [own] + [mirrored(own, 0, hop * (k // 2) + k % 2) for k in range(1, 4)]
    else:
        (plane,) = call(sum_kernel, [(half, F32)], [], arrived)
        own = lax.psum(plane, "seq", axis_index_groups=column_groups(hop)).astype(BF16)
        parts = [own, mirrored(own, 0, 1)]
    outs = call(
        functools.partial(finish_kernel, scale, hop, n_blocks),
        [((3, rows, width), F32), ((width, rows), F32)] * n_blocks,
        [((n_blocks, rows, lanes), F32)],
        parts,
    )
    return [outs[2 * i : 2 * i + 2] for i in range(n_blocks)]


def shards(
    inputs,
    cotangent,
    first_dilated_kernel,
    first_pointwise_weight,
    second_dilated_kernel,
    second_pointwise_weight,
):
    samples, rows, channels = inputs.shape
    width = first_pointwise_weight.shape[0]
    hop = DILATION_ONE // rows
    count = lax.axis_size("seq") // hop
    size = rows // count
    halves = 1
    step = size // halves
    part = rows // halves
    shifts = (step, step * (DILATION_TWO // DILATION_ONE))
    total_rows = samples * lax.axis_size("dp") * rows * lax.axis_size("seq")
    scale = 1.0 / math.sqrt(total_rows)
    k1t = jnp.swapaxes(first_dilated_kernel, 1, 2)
    k2t = jnp.swapaxes(second_dilated_kernel, 1, 2)

    (x_parts,) = to_columns(inputs.reshape(rows, channels), hop, 1)
    g_parts = to_columns(cotangent.reshape(rows, channels), hop, halves, x_parts[1:3])
    n_parts = len(x_parts)
    state = [
        ((halves, channels, part), BF16),
        ((halves, width, part), BF16),
        ((halves, part, channels), BF16),
        ((halves, part, width), BF16),
    ]
    saved = call(
        functools.partial(forward_kernel, shifts, hop, n_parts, halves),
        state * 2,
        [
            ((part, channels), BF16),
            ((part + 2 * shifts[0], channels), BF16),
            ((part + 2 * shifts[1], channels), BF16),
            ((TILE, channels), BF16),
            ((TILE, width), F32),
        ],
        list(x_parts) + [k1t, first_pointwise_weight, k2t],
        mib=16,
    )
    piece_shape = (g_parts[0][0].shape, BF16)
    part_shape = ((part, channels), BF16)
    grads_shape = ((channels, 4 * width), F32)
    quarter = ((2, channels // 4, 4 * width), BF16)

    def backward(half, g_in, saved, shift, kt, point, out_shapes, so_far, after=()):
        first, last = half == 0, half == halves - 1
        scratch = [part_shape, ((part + 2 * shift, width), BF16), part_shape]
        results = call(
            functools.partial(
                backward_kernel, shift, hop, half, len(g_in), len(out_shapes), first, last
            ),
            out_shapes + ([quarter, quarter] if last else [grads_shape]),
            scratch + ([grads_shape] if last else []),
            list(g_in) + list(saved) + [kt, point] + ([] if first else [so_far]),
            after,
            mib=16,
        )
        n = len(out_shapes)
        return results[:n], results[n:]

    grads2, grads1 = (None,), (None,)
    x_grads = []
    for half in range(halves):
        hidden_grad, grads2 = backward(
            half, g_parts[half], saved[4:], shifts[1], k2t, second_pointwise_weight,
            [part_shape], grads2[0],
        )
        outs, grads1 = backward(
            half, hidden_grad, saved[:4], shifts[0], k1t, first_pointwise_weight,
            [piece_shape] * n_parts, grads1[0],
        )
        x_grads.append(outs)
    back = []
    for outs in x_grads:
        if n_parts == 1:
            back.append(exchange_all(outs[0], hop))
        else:
            back += forward_pieces(outs, hop)
    if n_parts == 1:
        (input_grad,) = back
    else:
        (input_grad,) = call(
            functools.partial(collect_kernel, hop, halves), [((rows, channels), BF16)], [], back
        )
    if MERGED:
        (conv2, point2), (conv1, point1) = reduce_weights([grads2, grads1], hop, scale, back[1:])
    else:
        ((conv2, point2),) = reduce_weights([grads2], hop, scale, back[1:])
        ((conv1, point1),) = reduce_weights([grads1], hop, scale, back[1:])
    return input_grad.reshape(inputs.shape), conv1, point1, conv2, point2


def solution(mesh):
    return jax.shard_map(
        shards,
        mesh=mesh,
        in_specs=(P("dp", "seq", None), P("dp", "seq", None), P(), P(), P(), P()),
        out_specs=(
            P("dp", "seq", None),
            P(None, "dp", None),
            P(None, "dp"),
            P(None, "dp", None),
            P(None, "dp"),
        ),
        check_vma=False,
    )
```

```python
import functools
import math

import jax
import jax.numpy as jnp
from jax import lax
from jax.experimental import pallas as pl
from jax.experimental.pallas import tpu as pltpu
from jax.sharding import PartitionSpec as P

DILATION_ONE = 2048
DILATION_TWO = 4096
TILE = 256
CHUNK = 32
MAX_PERMUTES = 8
NEED = ((1,), (2,), (3,))
GATE = (1, 2,)
BF16 = jnp.bfloat16
F32 = jnp.float32
VMEM = pl.BlockSpec(memory_space=pltpu.VMEM)
ANY = pl.BlockSpec(memory_space=pl.ANY)


def gelu_parts(values):
    coeff = math.sqrt(2.0 / math.pi)
    square = values * values
    tanh_val = jnp.tanh(values * (coeff + (coeff * 0.044715) * square))
    half = 0.5 + 0.5 * tanh_val
    slope = half + half * (1.0 - tanh_val) * (values * (coeff + (3.0 * coeff * 0.044715) * square))
    return values * half, slope


def dot(left, right):
    return jnp.dot(left, right, preferred_element_type=F32)


def dot_nt(left, right):
    return lax.dot_general(left, right, (((1,), (1,)), ((), ())), preferred_element_type=F32)


def position(hop):
    return lax.axis_index("seq") // hop


def behind(me, k, count):
    return lax.rem(me + (count - k), count)


def ahead(me, k, count):
    return lax.rem(me + k, count)


def call(kernel, out_shapes, scratch, args, after=(), mib=8):
    n_args, n_after = len(args), len(after)

    def body(*refs):
        kernel(*refs[:n_args], *refs[n_args + n_after :])

    return pl.pallas_call(
        body,
        out_shape=[jax.ShapeDtypeStruct(s, d) for s, d in out_shapes],
        in_specs=[VMEM] * n_args + [ANY] * n_after,
        out_specs=[VMEM] * len(out_shapes),
        scratch_shapes=[pltpu.VMEM(s, d) for s, d in scratch],
        compiler_params=pltpu.CompilerParams(vmem_limit_bytes=mib << 20),
    )(*args, *after)


def cut_kernel(hop, block, *pieces):
    count = len(pieces)
    size = pieces[0].shape[0]
    me = position(hop)
    for k, piece in enumerate(pieces):
        at = pl.multiple_of(ahead(me, k, count) * size, size)
        piece[...] = block[pl.ds(at, size), :]


def place(parts, rows_ref, hop):
    if len(parts) == 1:
        rows_ref[...] = parts[0][...]
        return
    count = len(parts)
    size = rows_ref.shape[0] // count
    me = position(hop)
    for k, part in enumerate(parts):
        at = pl.multiple_of(behind(me, k, count) * size, size)
        rows_ref[pl.ds(at, size), :] = part[...]


def hand_out(rows_ref, parts, hop):
    if len(parts) == 1:
        parts[0][...] = rows_ref[...]
        return
    count = len(parts)
    size = rows_ref.shape[0] // count
    me = position(hop)
    for k, part in enumerate(parts):
        at = pl.multiple_of(ahead(me, k, count) * size, size)
        part[...] = rows_ref[pl.ds(at, size), :]


def tap_sum(padded_ref, shift, start, tile, weight_of, mm):
    total = mm(padded_ref[pl.ds(start + shift, tile), :], weight_of(1))
    rows = padded_ref.shape[0] - 2 * shift
    if start + tile > shift:
        total = total + mm(padded_ref[pl.ds(start, tile), :], weight_of(0))
    if start < rows - shift:
        total = total + mm(padded_ref[pl.ds(start + 2 * shift, tile), :], weight_of(2))
    return total


def clear_edges(padded_ref, shift):
    rows = padded_ref.shape[0]
    zeros = jnp.zeros((shift, padded_ref.shape[1]), padded_ref.dtype)
    padded_ref[pl.ds(0, shift), :] = zeros
    padded_ref[pl.ds(rows - shift, shift), :] = zeros


def forward_kernel(shifts, hop, count, *refs):
    parts = refs[:count]
    weights = refs[count : count + 3]
    outs = refs[count + 3 : count + 11]
    scratch = refs[count + 11 :]
    place(parts, scratch[0], hop)
    forward_rows(shifts, weights, outs, scratch)


def forward_rows(shifts, weights, outs, scratch):
    k1t, p1, k2t = weights
    act1_t, mid1_t, s_x, s_p1, act2_t, mid2_t, s_h, s_p2 = outs
    x_rows, pad1, pad2, wide, narrow = scratch
    rows = x_rows.shape[0]

    def activate(source, source_start, pad, shift, start, slope_ref):
        def step(i, carry):
            at = pl.multiple_of(i * CHUNK, CHUNK)
            value, slope = gelu_parts(source[pl.ds(source_start + at, CHUNK), :].astype(F32))
            pad[pl.ds(start + shift + at, CHUNK), :] = value.astype(BF16)
            slope_ref[pl.ds(start + at, CHUNK), :] = slope
            return carry

        lax.fori_loop(0, TILE // CHUNK, step, 0, unroll=2)

    def narrow_gelu(start, slope_ref):
        def step(i, carry):
            at = pl.multiple_of(i * CHUNK, CHUNK)
            value, slope = gelu_parts(narrow[pl.ds(at, CHUNK), :])
            narrow[pl.ds(at, CHUNK), :] = value
            slope_ref[pl.ds(start + at, CHUNK), :] = slope
            return carry

        lax.fori_loop(0, TILE // CHUNK, step, 0, unroll=2)

    clear_edges(pad1, shifts[0])
    clear_edges(pad2, shifts[1])
    for start in range(0, rows, TILE):
        activate(x_rows, start, pad1, shifts[0], start, s_x)
        act1_t[:, pl.ds(start, TILE)] = pad1[pl.ds(start + shifts[0], TILE), :].T
    for start in range(0, rows, TILE):
        narrow[...] = tap_sum(pad1, shifts[0], start, TILE, lambda k: k1t[k], dot_nt)
        narrow_gelu(start, s_p1)
        mid = narrow[...].astype(BF16)
        mid1_t[:, pl.ds(start, TILE)] = mid.T
        wide[...] = (x_rows[pl.ds(start, TILE), :].astype(F32) + dot(mid, p1[...])).astype(BF16)
        activate(wide, 0, pad2, shifts[1], start, s_h)
        act2_t[:, pl.ds(start, TILE)] = pad2[pl.ds(start + shifts[1], TILE), :].T
    for start in range(0, rows, TILE):
        narrow[...] = tap_sum(pad2, shifts[1], start, TILE, lambda k: k2t[k], dot_nt)
        narrow_gelu(start, s_p2)
        mid2_t[:, pl.ds(start, TILE)] = narrow[...].astype(BF16).T


def chain_kernel(shifts, hop, n_in, n_out, *refs):
    parts = refs[:n_in]
    s_x, s_p1, s_h, s_p2, k1t, p1, k2t, p2 = refs[n_in : n_in + 8]
    outs = refs[n_in + 8 : n_in + 8 + n_out]
    g2_rows, pad2, g1_rows, pad1, x_rows = refs[n_in + 8 + n_out :]
    place(parts, g2_rows, hop)
    backward_rows(shifts[1], g2_rows, pad2, s_p2, s_h, k2t, p2, g1_rows)
    backward_rows(shifts[0], g1_rows, pad1, s_p1, s_x, k1t, p1, x_rows)
    hand_out(x_rows, outs, hop)


def backward_rows(shift, g_rows, pad, s_pre, s_state, kt, point, x_rows):
    rows = g_rows.shape[0]
    clear_edges(pad, shift)
    for start in range(0, rows, TILE):
        mid_grad = dot_nt(g_rows[pl.ds(start, TILE), :], point[...])
        pad[pl.ds(start + shift, TILE), :] = (mid_grad * s_pre[pl.ds(start, TILE), :]).astype(BF16)
    for start in range(0, rows, TILE):
        act_grad = tap_sum(pad, shift, start, TILE, lambda k: kt[2 - k], dot)
        x_rows[pl.ds(start, TILE), :] = (
            g_rows[pl.ds(start, TILE), :].astype(F32) + act_grad * s_state[pl.ds(start, TILE), :]
        ).astype(BF16)


def weights_kernel(shifts, *refs):
    keep, send, grads = refs[-3:]
    size = keep.shape[2]
    core = lax.rem(lax.axis_index("dp"), 2)
    for i, shift in enumerate(shifts):
        act_t, mid_t, pad, g_rows = refs[4 * i : 4 * i + 4]
        rows = g_rows.shape[0]
        act = act_t[...]
        grads[...] = jnp.concatenate(
            [
                dot(act, pad[pl.ds(2 * shift, rows), :]),
                dot(act, pad[pl.ds(shift, rows), :]),
                dot(act, pad[pl.ds(0, rows), :]),
                dot(mid_t[...], g_rows[...]).T,
            ],
            axis=1,
        )
        for x_to in range(2):
            for target, parity in ((keep, core), (send, 1 - core)):
                rows_at = pl.multiple_of((2 * x_to + parity) * size, size)
                target[i, x_to] = grads[pl.ds(rows_at, size), :].astype(target.dtype)


def split_kernel(keep, received, *pieces):
    x_at = lax.axis_index("dp") // 2
    y_at = lax.rem(lax.axis_index("seq"), 2)
    size = pieces[0].shape[1]
    for k, piece in enumerate(pieces):
        x_to = lax.rem(x_at + k // 2, 2)
        rows = pl.ds(pl.multiple_of(lax.rem(y_at + k, 2) * size, size), size)
        for i in range(keep.shape[0]):
            total = keep[i, x_to, rows, :].astype(F32) + received[i, x_to, rows, :].astype(F32)
            piece[i] = total.astype(piece.dtype)


def sum_of(refs):
    total = refs[0][...].astype(F32)
    for ref in refs[1:]:
        total = total + ref[...].astype(F32)
    return total


def sum_kernel(*refs):
    refs[-1][...] = sum_of(refs[:-1]).astype(refs[-1].dtype)


def halve_kernel(hop, *refs):
    *parts, keep, send, total = refs
    total[...] = sum_of(parts)
    size = keep.shape[1]
    mine = lax.rem(position(hop), 2)
    for target, half in ((keep, mine), (send, 1 - mine)):
        target[...] = total[:, pl.ds(pl.multiple_of(half * size, size), size), :].astype(target.dtype)


def finish_kernel(scale, hop, n_blocks, *refs):
    parts, outs, rows = refs[: -2 * n_blocks - 1], refs[-2 * n_blocks - 1 : -1], refs[-1]
    z_at = lax.rem(position(hop), 2)
    y_at = lax.rem(lax.axis_index("seq"), 2)
    size = parts[0].shape[1]
    per_y = rows.shape[1] // 2
    for k, part in enumerate(parts):
        at = lax.rem(y_at + k, 2) * per_y
        if len(parts) > 2:
            at = at + lax.rem(z_at + k // 2, 2) * size
        rows[:, pl.ds(pl.multiple_of(at, size), size), :] = part[...].astype(F32) * scale
    for i in range(n_blocks):
        conv, point = outs[2 * i : 2 * i + 2]
        width = conv.shape[2]
        whole = rows[i]
        for k in range(3):
            conv[k] = whole[:, k * width : (k + 1) * width]
        point[...] = whole[:, 3 * width :].T


def collect_kernel(hop, *refs):
    place(refs[:-1], refs[-1], hop)


def send_ahead(block, hop, k):
    size = lax.axis_size("seq")
    count = size // hop
    route = [(i, ((i // hop + k) % count) * hop + i % hop) for i in range(size)]
    return lax.ppermute(block, "seq", route)


def mirrored(block, dp_bits, seq_bits):
    n_dp, n_seq = lax.axis_size("dp"), lax.axis_size("seq")
    route = [
        (i * n_seq + j, (i ^ dp_bits) * n_seq + (j ^ seq_bits))
        for i in range(n_dp)
        for j in range(n_seq)
    ]
    return lax.ppermute(block, ("dp", "seq"), route)


def column_groups(hop):
    size = lax.axis_size("seq")
    return [list(range(first, size, hop)) for first in range(hop)]


def exchange_all(block, hop):
    count = lax.axis_size("seq") // hop
    cut = block.reshape(count, -1, block.shape[-1])
    swapped = lax.all_to_all(cut, "seq", 0, 0, axis_index_groups=column_groups(hop), tiled=True)
    return swapped.reshape(block.shape)


def to_columns(block, hop, after=()):
    count = lax.axis_size("seq") // hop
    rows, channels = block.shape
    if count > MAX_PERMUTES:
        return [exchange_all(block, hop)]
    pieces = call(
        functools.partial(cut_kernel, hop), [((rows // count, channels), BF16)] * count, [], [block], mib=2
    )
    if after:
        pieces, _ = lax.optimization_barrier((pieces, list(after)))
    return forward_pieces(pieces, hop)


def forward_pieces(pieces, hop):
    return [pieces[0]] + [send_ahead(pieces[k], hop, k) for k in range(1, len(pieces))]


def once(block, after):
    return lax.optimization_barrier((block, after))[0]


def reduce_weights(keep, send, grads, hop, scale):
    n_blocks, _, rows, lanes = keep.shape
    width = lanes // 4
    count = lax.axis_size("seq") // hop
    half = (n_blocks, rows // 2, lanes)
    fourth = (n_blocks, rows // 4, lanes)
    received = mirrored(send, 1, 0)
    back = dict.fromkeys(range(count))

    def send_home(ks, after=None):
        for k in ks:
            back[k] = send_ahead(grads[k] if after is None else once(grads[k], after), hop, k)
        return [back[k] for k in ks]

    if count == 4:
        back[0] = grads[0]
        send_home((1, 2, 3))
    pieces = call(split_kernel, [(half, F32)] + [(half, BF16)] * 3, [], [keep, received])
    arrived = [pieces[0]] + [mirrored(pieces[k], 2 * (k // 2), k % 2) for k in range(1, 4)]
    if count == 4:
        keep, send = call(
            functools.partial(halve_kernel, hop), [(fourth, F32), (fourth, BF16)], [(half, F32)], arrived,
            [back[k] for k in NEED[0]],
        )
        (pair,) = call(sum_kernel, [(fourth, BF16)], [], [keep, mirrored(send, 0, hop)], [back[k] for k in NEED[1]])
        (own,) = call(sum_kernel, [(fourth, BF16)], [], [pair, mirrored(pair, 0, 2 * hop)], [back[k] for k in NEED[2]])
        parts = [own] + [mirrored(own, 0, hop * (k // 2) + k % 2) for k in range(1, 4)]
        back = [back[k] for k in range(count)]
    else:
        (plane,) = call(sum_kernel, [(half, F32)], [], arrived)
        own = lax.psum(plane, "seq", axis_index_groups=column_groups(hop)).astype(BF16)
        parts = [own, mirrored(own, 0, 1)]
        back = [exchange_all(grads[0], hop)] if len(grads) == 1 else forward_pieces(grads, hop)
    outs = call(
        functools.partial(finish_kernel, scale, hop, n_blocks),
        [((3, rows, width), F32), ((width, rows), F32)] * n_blocks,
        [((n_blocks, rows, lanes), F32)],
        parts,
    )
    return back, [outs[2 * i : 2 * i + 2] for i in range(n_blocks)]


def shards(
    inputs,
    cotangent,
    first_dilated_kernel,
    first_pointwise_weight,
    second_dilated_kernel,
    second_pointwise_weight,
):
    samples, rows, channels = inputs.shape
    width = first_pointwise_weight.shape[0]
    hop = DILATION_ONE // rows
    size = rows // (lax.axis_size("seq") // hop)
    shifts = (size, size * (DILATION_TWO // DILATION_ONE))
    total_rows = samples * lax.axis_size("dp") * rows * lax.axis_size("seq")
    scale = 1.0 / math.sqrt(total_rows)
    k1t = jnp.swapaxes(first_dilated_kernel, 1, 2)
    k2t = jnp.swapaxes(second_dilated_kernel, 1, 2)
    p1, p2 = first_pointwise_weight, second_pointwise_weight

    x_parts = to_columns(inputs.reshape(rows, channels), hop)
    g_parts = to_columns(cotangent.reshape(rows, channels), hop, [x_parts[k] for k in GATE if k < len(x_parts)])
    n_parts = len(x_parts)
    whole = ((rows, channels), BF16)
    pads = [((rows + 2 * shift, width), BF16) for shift in shifts]
    state = [((channels, rows), BF16), ((width, rows), BF16), ((rows, channels), F32), ((rows, width), F32)]
    act1_t, mid1_t, s_x, s_p1, act2_t, mid2_t, s_h, s_p2 = call(
        functools.partial(forward_kernel, shifts, hop, n_parts),
        state * 2,
        [
            whole,
            ((rows + 2 * shifts[0], channels), BF16),
            ((rows + 2 * shifts[1], channels), BF16),
            ((TILE, channels), BF16),
            ((TILE, width), F32),
        ],
        list(x_parts) + [k1t, p1, k2t],
        mib=16,
    )
    *x_grads, g2_rows, pad2, g1_rows, pad1 = call(
        functools.partial(chain_kernel, shifts, hop, n_parts, n_parts),
        [(x_parts[0].shape, BF16)] * n_parts + [whole, pads[1], whole, pads[0]],
        [whole],
        list(g_parts) + [s_x, s_p1, s_h, s_p2, k1t, p1, k2t, p2],
        mib=16,
    )
    quarters = ((2, 2, channels // 4, 4 * width), BF16)
    keep, send = call(
        functools.partial(weights_kernel, (shifts[1], shifts[0])),
        [quarters, quarters],
        [((channels, 4 * width), F32)],
        [act2_t, mid2_t, pad2, g2_rows, act1_t, mid1_t, pad1, g1_rows],
        mib=16,
    )
    back, ((conv2, point2), (conv1, point1)) = reduce_weights(keep, send, x_grads, hop, scale)
    if n_parts == 1:
        (input_grad,) = back
    else:
        (input_grad,) = call(functools.partial(collect_kernel, hop), [whole], [], back)
    return input_grad.reshape(inputs.shape), conv1, point1, conv2, point2


def solution(mesh):
    return jax.shard_map(
        shards,
        mesh=mesh,
        in_specs=(P("dp", "seq", None), P("dp", "seq", None), P(), P(), P(), P()),
        out_specs=(
            P("dp", "seq", None),
            P(None, "dp", None),
            P(None, "dp"),
            P(None, "dp", None),
            P(None, "dp"),
        ),
        check_vma=False,
    )
```

```python
import functools
import math

import jax
import jax.numpy as jnp
from jax import lax
from jax.experimental import pallas as pl
from jax.experimental.pallas import tpu as pltpu
from jax.sharding import PartitionSpec as P

DILATION_ONE = 2048
DILATION_TWO = 4096
TILE = 256
CHUNK = 32
MAX_PERMUTES = 4
NEED = ((1,), (2,), (3,))
ORDER = (2, 3, 1)
GATE = (3,)
BF16 = jnp.bfloat16
F32 = jnp.float32
VMEM = pl.BlockSpec(memory_space=pltpu.VMEM)
ANY = pl.BlockSpec(memory_space=pl.ANY)


def gelu_parts(values):
    coeff = math.sqrt(2.0 / math.pi)
    square = values * values
    tanh_val = jnp.tanh(values * (coeff + (coeff * 0.044715) * square))
    half = 0.5 + 0.5 * tanh_val
    slope = half + half * (1.0 - tanh_val) * (values * (coeff + (3.0 * coeff * 0.044715) * square))
    return values * half, slope


def dot(left, right):
    return jnp.dot(left, right, preferred_element_type=F32)


def dot_nt(left, right):
    return lax.dot_general(left, right, (((1,), (1,)), ((), ())), preferred_element_type=F32)


def position(hop):
    return lax.axis_index("seq") // hop


def call(kernel, out_shapes, scratch, args, after=(), mib=8):
    n_args, n_after = len(args), len(after)

    def body(*refs):
        kernel(*refs[:n_args], *refs[n_args + n_after :])

    return pl.pallas_call(
        body,
        out_shape=[jax.ShapeDtypeStruct(s, d) for s, d in out_shapes],
        in_specs=[VMEM] * n_args + [ANY] * n_after,
        out_specs=[VMEM] * len(out_shapes),
        scratch_shapes=[pltpu.VMEM(s, d) for s, d in scratch],
        compiler_params=pltpu.CompilerParams(vmem_limit_bytes=mib << 20),
    )(*args, *after)


def cut_kernel(hop, block, *pieces):
    count = len(pieces)
    size = pieces[0].shape[0]
    me = position(hop)
    for k, piece in enumerate(pieces):
        at = pl.multiple_of((me ^ k) * size, size)
        piece[...] = block[pl.ds(at, size), :]


def place(parts, rows_ref, hop):
    if len(parts) == 1:
        rows_ref[...] = parts[0][...]
        return
    count = len(parts)
    size = rows_ref.shape[0] // count
    me = position(hop)
    for k, part in enumerate(parts):
        at = pl.multiple_of((me ^ k) * size, size)
        rows_ref[pl.ds(at, size), :] = part[...]


def hand_out(rows_ref, parts, hop):
    if len(parts) == 1:
        parts[0][...] = rows_ref[...]
        return
    count = len(parts)
    size = rows_ref.shape[0] // count
    me = position(hop)
    for k, part in enumerate(parts):
        at = pl.multiple_of(lax.rem(me + k, count) * size, size)
        part[...] = rows_ref[pl.ds(at, size), :]


def tap_sum(padded_ref, shift, start, tile, weight_of, mm):
    total = mm(padded_ref[pl.ds(start + shift, tile), :], weight_of(1))
    rows = padded_ref.shape[0] - 2 * shift
    if start + tile > shift:
        total = total + mm(padded_ref[pl.ds(start, tile), :], weight_of(0))
    if start < rows - shift:
        total = total + mm(padded_ref[pl.ds(start + 2 * shift, tile), :], weight_of(2))
    return total


def clear_edges(padded_ref, shift):
    rows = padded_ref.shape[0]
    zeros = jnp.zeros((shift, padded_ref.shape[1]), padded_ref.dtype)
    padded_ref[pl.ds(0, shift), :] = zeros
    padded_ref[pl.ds(rows - shift, shift), :] = zeros


def forward_kernel(shifts, hop, count, *refs):
    parts = refs[:count]
    weights = refs[count : count + 3]
    outs = refs[count + 3 : count + 11]
    scratch = refs[count + 11 :]
    place(parts, scratch[0], hop)
    forward_rows(shifts, weights, outs, scratch)


def forward_rows(shifts, weights, outs, scratch):
    k1t, p1, k2t = weights
    act1_t, mid1_t, s_x, s_p1, act2_t, mid2_t, s_h, s_p2 = outs
    x_rows, pad1, pad2, wide, narrow = scratch
    rows = x_rows.shape[0]

    def activate(source, source_start, pad, shift, start, slope_ref):
        def step(i, carry):
            at = pl.multiple_of(i * CHUNK, CHUNK)
            value, slope = gelu_parts(source[pl.ds(source_start + at, CHUNK), :].astype(F32))
            pad[pl.ds(start + shift + at, CHUNK), :] = value.astype(BF16)
            slope_ref[pl.ds(start + at, CHUNK), :] = slope
            return carry

        lax.fori_loop(0, TILE // CHUNK, step, 0, unroll=2)

    def narrow_gelu(start, slope_ref):
        def step(i, carry):
            at = pl.multiple_of(i * CHUNK, CHUNK)
            value, slope = gelu_parts(narrow[pl.ds(at, CHUNK), :])
            narrow[pl.ds(at, CHUNK), :] = value
            slope_ref[pl.ds(start + at, CHUNK), :] = slope
            return carry

        lax.fori_loop(0, TILE // CHUNK, step, 0, unroll=2)

    clear_edges(pad1, shifts[0])
    clear_edges(pad2, shifts[1])
    for start in range(0, rows, TILE):
        activate(x_rows, start, pad1, shifts[0], start, s_x)
        act1_t[:, pl.ds(start, TILE)] = pad1[pl.ds(start + shifts[0], TILE), :].T
    for start in range(0, rows, TILE):
        narrow[...] = tap_sum(pad1, shifts[0], start, TILE, lambda k: k1t[k], dot_nt)
        narrow_gelu(start, s_p1)
        mid = narrow[...].astype(BF16)
        mid1_t[:, pl.ds(start, TILE)] = mid.T
        wide[...] = (x_rows[pl.ds(start, TILE), :].astype(F32) + dot(mid, p1[...])).astype(BF16)
        activate(wide, 0, pad2, shifts[1], start, s_h)
        act2_t[:, pl.ds(start, TILE)] = pad2[pl.ds(start + shifts[1], TILE), :].T
    for start in range(0, rows, TILE):
        narrow[...] = tap_sum(pad2, shifts[1], start, TILE, lambda k: k2t[k], dot_nt)
        narrow_gelu(start, s_p2)
        mid2_t[:, pl.ds(start, TILE)] = narrow[...].astype(BF16).T


def chain_kernel(shifts, hop, n_in, n_out, *refs):
    parts = refs[:n_in]
    s_x, s_p1, s_h, s_p2, k1t, p1, k2t, p2 = refs[n_in : n_in + 8]
    outs = refs[n_in + 8 : n_in + 8 + n_out]
    g2_rows, pad2, g1_rows, pad1, x_rows = refs[n_in + 8 + n_out :]
    place(parts, g2_rows, hop)
    backward_rows(shifts[1], g2_rows, pad2, s_p2, s_h, k2t, p2, g1_rows)
    backward_rows(shifts[0], g1_rows, pad1, s_p1, s_x, k1t, p1, x_rows)
    hand_out(x_rows, outs, hop)


def backward_rows(shift, g_rows, pad, s_pre, s_state, kt, point, x_rows):
    rows = g_rows.shape[0]
    clear_edges(pad, shift)
    for start in range(0, rows, TILE):
        mid_grad = dot_nt(g_rows[pl.ds(start, TILE), :], point[...])
        pad[pl.ds(start + shift, TILE), :] = (mid_grad * s_pre[pl.ds(start, TILE), :]).astype(BF16)
    for start in range(0, rows, TILE):
        act_grad = tap_sum(pad, shift, start, TILE, lambda k: kt[2 - k], dot)
        x_rows[pl.ds(start, TILE), :] = (
            g_rows[pl.ds(start, TILE), :].astype(F32) + act_grad * s_state[pl.ds(start, TILE), :]
        ).astype(BF16)


def weights_kernel(shifts, *refs):
    keep, send, grads = refs[-3:]
    size = keep.shape[2]
    core = lax.rem(lax.axis_index("dp"), 2)
    for i, shift in enumerate(shifts):
        act_t, mid_t, pad, g_rows = refs[4 * i : 4 * i + 4]
        rows = g_rows.shape[0]
        act = act_t[...]
        grads[...] = jnp.concatenate(
            [
                dot(act, pad[pl.ds(2 * shift, rows), :]),
                dot(act, pad[pl.ds(shift, rows), :]),
                dot(act, pad[pl.ds(0, rows), :]),
                dot(mid_t[...], g_rows[...]).T,
            ],
            axis=1,
        )
        for x_to in range(2):
            for target, parity in ((keep, core), (send, 1 - core)):
                rows_at = pl.multiple_of((2 * x_to + parity) * size, size)
                target[i, x_to] = grads[pl.ds(rows_at, size), :].astype(target.dtype)


def split_kernel(keep, received, *pieces):
    x_at = lax.axis_index("dp") // 2
    y_at = lax.rem(lax.axis_index("seq"), 2)
    size = pieces[0].shape[1]
    for k, piece in enumerate(pieces):
        x_to = lax.rem(x_at + k // 2, 2)
        rows = pl.ds(pl.multiple_of(lax.rem(y_at + k, 2) * size, size), size)
        for i in range(keep.shape[0]):
            total = keep[i, x_to, rows, :].astype(F32) + received[i, x_to, rows, :].astype(F32)
            piece[i] = total.astype(piece.dtype)


def sum_of(refs):
    total = refs[0][...].astype(F32)
    for ref in refs[1:]:
        total = total + ref[...].astype(F32)
    return total


def sum_kernel(*refs):
    refs[-1][...] = sum_of(refs[:-1]).astype(refs[-1].dtype)


def halve_kernel(hop, *refs):
    *parts, keep, send, total = refs
    total[...] = sum_of(parts)
    size = keep.shape[1]
    mine = lax.rem(position(hop), 2)
    for target, half in ((keep, mine), (send, 1 - mine)):
        target[...] = total[:, pl.ds(pl.multiple_of(half * size, size), size), :].astype(target.dtype)


def finish_kernel(scale, hop, n_blocks, *refs):
    parts, outs, rows = refs[: -2 * n_blocks - 1], refs[-2 * n_blocks - 1 : -1], refs[-1]
    z_at = lax.rem(position(hop), 2)
    y_at = lax.rem(lax.axis_index("seq"), 2)
    size = parts[0].shape[1]
    per_y = rows.shape[1] // 2
    for k, part in enumerate(parts):
        at = lax.rem(y_at + k, 2) * per_y
        if len(parts) > 2:
            at = at + lax.rem(z_at + k // 2, 2) * size
        rows[:, pl.ds(pl.multiple_of(at, size), size), :] = part[...].astype(F32) * scale
    for i in range(n_blocks):
        conv, point = outs[2 * i : 2 * i + 2]
        width = conv.shape[2]
        whole = rows[i]
        for k in range(3):
            conv[k] = whole[:, k * width : (k + 1) * width]
        point[...] = whole[:, 3 * width :].T


def collect_kernel(hop, *refs):
    *parts, rows_ref = refs
    count = len(parts)
    size = rows_ref.shape[0] // count
    me = position(hop)
    for k, part in enumerate(parts):
        at = pl.multiple_of(lax.rem(me + (count - k), count) * size, size)
        rows_ref[pl.ds(at, size), :] = part[...]


def send_ahead(block, hop, k):
    size = lax.axis_size("seq")
    count = size // hop
    route = [(i, ((i // hop + k) % count) * hop + i % hop) for i in range(size)]
    return lax.ppermute(block, "seq", route)


def mirrored(block, dp_bits, seq_bits):
    n_dp, n_seq = lax.axis_size("dp"), lax.axis_size("seq")
    route = [
        (i * n_seq + j, (i ^ dp_bits) * n_seq + (j ^ seq_bits))
        for i in range(n_dp)
        for j in range(n_seq)
    ]
    return lax.ppermute(block, ("dp", "seq"), route)


def column_groups(hop):
    size = lax.axis_size("seq")
    return [list(range(first, size, hop)) for first in range(hop)]


def exchange_all(block, hop):
    count = lax.axis_size("seq") // hop
    cut = block.reshape(count, -1, block.shape[-1])
    swapped = lax.all_to_all(cut, "seq", 0, 0, axis_index_groups=column_groups(hop), tiled=True)
    return swapped.reshape(block.shape)


def to_columns(block, hop, after=()):
    count = lax.axis_size("seq") // hop
    rows, channels = block.shape
    if count != MAX_PERMUTES:
        return [exchange_all(block, hop)]
    pieces = call(
        functools.partial(cut_kernel, hop), [((rows // count, channels), BF16)] * count, [], [block], mib=2
    )
    if after:
        pieces, _ = lax.optimization_barrier((pieces, list(after)))
    return forward_pieces(pieces, hop)


def forward_pieces(pieces, hop):
    sent = {k: mirrored(pieces[k], 0, k * hop) for k in ORDER[: len(pieces) - 1]}
    return [pieces[0]] + [sent[k] for k in sorted(sent)]


def reduce_weights(keep, send, grads, hop, scale):
    n_blocks, _, rows, lanes = keep.shape
    width = lanes // 4
    count = lax.axis_size("seq") // hop
    half = (n_blocks, rows // 2, lanes)
    fourth = (n_blocks, rows // 4, lanes)
    received = mirrored(send, 1, 0)
    back = {}


    if count == MAX_PERMUTES:
        back[0] = grads[0]
        for k in range(1, count):
            back[k] = send_ahead(grads[k], hop, k)
    pieces = call(split_kernel, [(half, F32)] + [(half, BF16)] * 3, [], [keep, received])
    arrived = [pieces[0]] + [mirrored(pieces[k], 2 * (k // 2), k % 2) for k in range(1, 4)]
    if count == MAX_PERMUTES:
        keep, send = call(
            functools.partial(halve_kernel, hop), [(fourth, F32), (fourth, BF16)], [(half, F32)], arrived,
            [back[k] for k in NEED[0]],
        )
        (pair,) = call(sum_kernel, [(fourth, BF16)], [], [keep, mirrored(send, 0, hop)], [back[k] for k in NEED[1]])
        (own,) = call(sum_kernel, [(fourth, BF16)], [], [pair, mirrored(pair, 0, 2 * hop)], [back[k] for k in NEED[2]])
        parts = [own] + [mirrored(own, 0, hop * (k // 2) + k % 2) for k in range(1, 4)]
        back = [back[k] for k in range(count)]
    else:
        (plane,) = call(sum_kernel, [(half, F32)], [], arrived)
        own = lax.psum(plane, "seq", axis_index_groups=column_groups(hop)).astype(BF16)
        parts = [own, mirrored(own, 0, 1)]
        back = [exchange_all(grads[0], hop)]
    outs = call(
        functools.partial(finish_kernel, scale, hop, n_blocks),
        [((3, rows, width), F32), ((width, rows), F32)] * n_blocks,
        [((n_blocks, rows, lanes), F32)],
        parts,
    )
    return back, [outs[2 * i : 2 * i + 2] for i in range(n_blocks)]


def shards(
    inputs,
    cotangent,
    first_dilated_kernel,
    first_pointwise_weight,
    second_dilated_kernel,
    second_pointwise_weight,
):
    samples, rows, channels = inputs.shape
    width = first_pointwise_weight.shape[0]
    hop = DILATION_ONE // rows
    size = rows // (lax.axis_size("seq") // hop)
    shifts = (size, size * (DILATION_TWO // DILATION_ONE))
    total_rows = samples * lax.axis_size("dp") * rows * lax.axis_size("seq")
    scale = 1.0 / math.sqrt(total_rows)
    k1t = jnp.swapaxes(first_dilated_kernel, 1, 2)
    k2t = jnp.swapaxes(second_dilated_kernel, 1, 2)
    p1, p2 = first_pointwise_weight, second_pointwise_weight

    x_parts = to_columns(inputs.reshape(rows, channels), hop)
    g_parts = to_columns(cotangent.reshape(rows, channels), hop, [x_parts[k] for k in GATE if k < len(x_parts)])
    n_parts = len(x_parts)
    whole = ((rows, channels), BF16)
    pads = [((rows + 2 * shift, width), BF16) for shift in shifts]
    state = [((channels, rows), BF16), ((width, rows), BF16), ((rows, channels), F32), ((rows, width), F32)]
    act1_t, mid1_t, s_x, s_p1, act2_t, mid2_t, s_h, s_p2 = call(
        functools.partial(forward_kernel, shifts, hop, n_parts),
        state * 2,
        [
            whole,
            ((rows + 2 * shifts[0], channels), BF16),
            ((rows + 2 * shifts[1], channels), BF16),
            ((TILE, channels), BF16),
            ((TILE, width), F32),
        ],
        list(x_parts) + [k1t, p1, k2t],
        mib=16,
    )
    *x_grads, g2_rows, pad2, g1_rows, pad1 = call(
        functools.partial(chain_kernel, shifts, hop, n_parts, n_parts),
        [(x_parts[0].shape, BF16)] * n_parts + [whole, pads[1], whole, pads[0]],
        [whole],
        list(g_parts) + [s_x, s_p1, s_h, s_p2, k1t, p1, k2t, p2],
        mib=16,
    )
    quarters = ((2, 2, channels // 4, 4 * width), BF16)
    keep, send = call(
        functools.partial(weights_kernel, (shifts[1], shifts[0])),
        [quarters, quarters],
        [((channels, 4 * width), F32)],
        [act2_t, mid2_t, pad2, g2_rows, act1_t, mid1_t, pad1, g1_rows],
        mib=16,
    )
    back, ((conv2, point2), (conv1, point1)) = reduce_weights(keep, send, x_grads, hop, scale)
    if n_parts == 1:
        (input_grad,) = back
    else:
        (input_grad,) = call(functools.partial(collect_kernel, hop), [whole], [], back)
    return input_grad.reshape(inputs.shape), conv1, point1, conv2, point2


def solution(mesh):
    return jax.shard_map(
        shards,
        mesh=mesh,
        in_specs=(P("dp", "seq", None), P("dp", "seq", None), P(), P(), P(), P()),
        out_specs=(
            P("dp", "seq", None),
            P(None, "dp", None),
            P(None, "dp"),
            P(None, "dp", None),
            P(None, "dp"),
        ),
        check_vma=False,
    )
```

```python
import functools
import math

import jax
import jax.numpy as jnp
from jax import lax
from jax.experimental import pallas as pl
from jax.experimental.pallas import tpu as pltpu
from jax.sharding import PartitionSpec as P

DILATION_ONE = 2048
DILATION_TWO = 4096
TILE = 256
CHUNK = 32
MAX_PERMUTES = 4
NEED = ((1,), (2,), (3,))
ORDER = (2, 3, 1)
GATE = (3,)
BF16 = jnp.bfloat16
F32 = jnp.float32
VMEM = pl.BlockSpec(memory_space=pltpu.VMEM)
ANY = pl.BlockSpec(memory_space=pl.ANY)


def gelu_parts(values):
    coeff = math.sqrt(2.0 / math.pi)
    square = values * values
    tanh_val = jnp.tanh(values * (coeff + (coeff * 0.044715) * square))
    half = 0.5 + 0.5 * tanh_val
    slope = half + half * (1.0 - tanh_val) * (values * (coeff + (3.0 * coeff * 0.044715) * square))
    return values * half, slope


def dot(left, right):
    return jnp.dot(left, right, preferred_element_type=F32)


def dot_nt(left, right):
    return lax.dot_general(left, right, (((1,), (1,)), ((), ())), preferred_element_type=F32)


def position(hop):
    return lax.axis_index("seq") // hop


def call(kernel, out_shapes, scratch, args, after=(), mib=8):
    n_args, n_after = len(args), len(after)

    def body(*refs):
        kernel(*refs[:n_args], *refs[n_args + n_after :])

    return pl.pallas_call(
        body,
        out_shape=[jax.ShapeDtypeStruct(s, d) for s, d in out_shapes],
        in_specs=[VMEM] * n_args + [ANY] * n_after,
        out_specs=[VMEM] * len(out_shapes),
        scratch_shapes=[pltpu.VMEM(s, d) for s, d in scratch],
        compiler_params=pltpu.CompilerParams(vmem_limit_bytes=mib << 20),
    )(*args, *after)


def cut_kernel(hop, block, *pieces):
    count = len(pieces)
    size = pieces[0].shape[0]
    me = position(hop)
    for k, piece in enumerate(pieces):
        at = pl.multiple_of((me ^ k) * size, size)
        piece[...] = block[pl.ds(at, size), :]


def place(parts, rows_ref, hop):
    if len(parts) == 1:
        rows_ref[...] = parts[0][...]
        return
    count = len(parts)
    size = rows_ref.shape[0] // count
    me = position(hop)
    for k, part in enumerate(parts):
        at = pl.multiple_of((me ^ k) * size, size)
        rows_ref[pl.ds(at, size), :] = part[...]


def hand_out(rows_ref, parts, hop):
    if len(parts) == 1:
        parts[0][...] = rows_ref[...]
        return
    count = len(parts)
    size = rows_ref.shape[0] // count
    me = position(hop)
    for k, part in enumerate(parts):
        at = pl.multiple_of(lax.rem(me + k, count) * size, size)
        part[...] = rows_ref[pl.ds(at, size), :]


def tap_sum(padded_ref, shift, start, tile, weight_of, mm):
    total = mm(padded_ref[pl.ds(start + shift, tile), :], weight_of(1))
    rows = padded_ref.shape[0] - 2 * shift
    if start + tile > shift:
        total = total + mm(padded_ref[pl.ds(start, tile), :], weight_of(0))
    if start < rows - shift:
        total = total + mm(padded_ref[pl.ds(start + 2 * shift, tile), :], weight_of(2))
    return total


def clear_edges(padded_ref, shift):
    rows = padded_ref.shape[0]
    zeros = jnp.zeros((shift, padded_ref.shape[1]), padded_ref.dtype)
    padded_ref[pl.ds(0, shift), :] = zeros
    padded_ref[pl.ds(rows - shift, shift), :] = zeros


def forward_kernel(shifts, hop, count, *refs):
    parts = refs[:count]
    weights = refs[count : count + 3]
    outs = refs[count + 3 : count + 11]
    scratch = refs[count + 11 :]
    place(parts, scratch[0], hop)
    forward_rows(shifts, weights, outs, scratch)


def forward_rows(shifts, weights, outs, scratch):
    k1t, p1, k2t = weights
    act1_t, mid1_t, s_x, s_p1, act2_t, mid2_t, s_h, s_p2 = outs
    x_rows, pad1, pad2, wide, narrow = scratch
    rows = x_rows.shape[0]

    def activate(source, source_start, pad, shift, start, slope_ref):
        def step(i, carry):
            at = pl.multiple_of(i * CHUNK, CHUNK)
            value, slope = gelu_parts(source[pl.ds(source_start + at, CHUNK), :].astype(F32))
            pad[pl.ds(start + shift + at, CHUNK), :] = value.astype(BF16)
            slope_ref[pl.ds(start + at, CHUNK), :] = slope
            return carry

        lax.fori_loop(0, TILE // CHUNK, step, 0, unroll=2)

    def narrow_gelu(start, slope_ref):
        def step(i, carry):
            at = pl.multiple_of(i * CHUNK, CHUNK)
            value, slope = gelu_parts(narrow[pl.ds(at, CHUNK), :])
            narrow[pl.ds(at, CHUNK), :] = value
            slope_ref[pl.ds(start + at, CHUNK), :] = slope
            return carry

        lax.fori_loop(0, TILE // CHUNK, step, 0, unroll=2)

    clear_edges(pad1, shifts[0])
    clear_edges(pad2, shifts[1])
    for start in range(0, rows, TILE):
        activate(x_rows, start, pad1, shifts[0], start, s_x)
        act1_t[:, pl.ds(start, TILE)] = pad1[pl.ds(start + shifts[0], TILE), :].T
    for start in range(0, rows, TILE):
        narrow[...] = tap_sum(pad1, shifts[0], start, TILE, lambda k: k1t[k], dot_nt)
        narrow_gelu(start, s_p1)
        mid = narrow[...].astype(BF16)
        mid1_t[:, pl.ds(start, TILE)] = mid.T
        wide[...] = (x_rows[pl.ds(start, TILE), :].astype(F32) + dot(mid, p1[...])).astype(BF16)
        activate(wide, 0, pad2, shifts[1], start, s_h)
        act2_t[:, pl.ds(start, TILE)] = pad2[pl.ds(start + shifts[1], TILE), :].T
    for start in range(0, rows, TILE):
        narrow[...] = tap_sum(pad2, shifts[1], start, TILE, lambda k: k2t[k], dot_nt)
        narrow_gelu(start, s_p2)
        mid2_t[:, pl.ds(start, TILE)] = narrow[...].astype(BF16).T


def chain_kernel(shifts, hop, n_in, *refs):
    parts = refs[:n_in]
    s_p1, s_h, s_p2, k2t, p1, p2, act1_t, mid1_t, act2_t, mid2_t = refs[n_in : n_in + 10]
    s_x, k1t = refs[n_in + 10 : n_in + 12]
    outs = refs[n_in + 12 : -8]
    keep, send, g1_rows, pad1, g2_rows, pad2, grads, x_rows = refs[-8:]
    place(parts, g2_rows, hop)
    middle_rows(shifts[1], g2_rows, pad2, s_p2, p2)
    outer_rows(shifts[1], g2_rows, pad2, s_h, k2t, g1_rows)
    middle_rows(shifts[0], g1_rows, pad1, s_p1, p1)
    weights_kernel(
        shifts[::-1], act2_t, mid2_t, pad2, g2_rows, act1_t, mid1_t, pad1, g1_rows, keep, send, grads
    )
    outer_rows(shifts[0], g1_rows, pad1, s_x, k1t, x_rows)
    hand_out(x_rows, outs, hop)


def middle_rows(shift, g_rows, pad, s_pre, point):
    clear_edges(pad, shift)
    for start in range(0, g_rows.shape[0], TILE):
        mid_grad = dot_nt(g_rows[pl.ds(start, TILE), :], point[...])
        pad[pl.ds(start + shift, TILE), :] = (mid_grad * s_pre[pl.ds(start, TILE), :]).astype(BF16)


def outer_rows(shift, g_rows, pad, s_state, kt, x_rows):
    for start in range(0, g_rows.shape[0], TILE):
        act_grad = tap_sum(pad, shift, start, TILE, lambda k: kt[2 - k], dot)
        x_rows[pl.ds(start, TILE), :] = (
            g_rows[pl.ds(start, TILE), :].astype(F32) + act_grad * s_state[pl.ds(start, TILE), :]
        ).astype(BF16)


def weights_kernel(shifts, *refs):
    keep, send, grads = refs[-3:]
    size = keep.shape[2]
    core = lax.rem(lax.axis_index("dp"), 2)
    for i, shift in enumerate(shifts):
        act_t, mid_t, pad, g_rows = refs[4 * i : 4 * i + 4]
        rows = g_rows.shape[0]
        act = act_t[...]
        near = rows - shift if shift % 128 == 0 else rows
        grads[...] = jnp.concatenate(
            [
                dot(act[:, :near], pad[pl.ds(2 * shift, near), :]),
                dot(act, pad[pl.ds(shift, rows), :]),
                dot(act[:, rows - near :], pad[pl.ds(rows - near, near), :]),
                dot(mid_t[...], g_rows[...]).T,
            ],
            axis=1,
        )
        for x_to in range(2):
            for target, parity in ((keep, core), (send, 1 - core)):
                rows_at = pl.multiple_of((2 * x_to + parity) * size, size)
                target[i, x_to] = grads[pl.ds(rows_at, size), :].astype(target.dtype)


def split_kernel(keep, received, *pieces):
    x_at = lax.axis_index("dp") // 2
    y_at = lax.rem(lax.axis_index("seq"), 2)
    size = pieces[0].shape[1]
    for k, piece in enumerate(pieces):
        x_to = lax.rem(x_at + k // 2, 2)
        rows = pl.ds(pl.multiple_of(lax.rem(y_at + k, 2) * size, size), size)
        for i in range(keep.shape[0]):
            total = keep[i, x_to, rows, :].astype(F32) + received[i, x_to, rows, :].astype(F32)
            piece[i] = total.astype(piece.dtype)


def sum_of(refs):
    total = refs[0][...].astype(F32)
    for ref in refs[1:]:
        total = total + ref[...].astype(F32)
    return total


def sum_kernel(*refs):
    refs[-1][...] = sum_of(refs[:-1]).astype(refs[-1].dtype)


def halve_kernel(hop, *refs):
    *parts, keep, send, total = refs
    total[...] = sum_of(parts)
    size = keep.shape[1]
    mine = lax.rem(position(hop), 2)
    for target, half in ((keep, mine), (send, 1 - mine)):
        target[...] = total[:, pl.ds(pl.multiple_of(half * size, size), size), :].astype(target.dtype)


def finish_kernel(scale, hop, n_blocks, *refs):
    parts, outs, rows = refs[: -2 * n_blocks - 1], refs[-2 * n_blocks - 1 : -1], refs[-1]
    z_at = lax.rem(position(hop), 2)
    y_at = lax.rem(lax.axis_index("seq"), 2)
    size = parts[0].shape[1]
    per_y = rows.shape[1] // 2
    for k, part in enumerate(parts):
        at = lax.rem(y_at + k, 2) * per_y
        if len(parts) > 2:
            at = at + lax.rem(z_at + k // 2, 2) * size
        rows[:, pl.ds(pl.multiple_of(at, size), size), :] = part[...].astype(F32) * scale
    for i in range(n_blocks):
        conv, point = outs[2 * i : 2 * i + 2]
        width = conv.shape[2]
        whole = rows[i]
        for k in range(3):
            conv[k] = whole[:, k * width : (k + 1) * width]
        point[...] = whole[:, 3 * width :].T


def collect_kernel(hop, *refs):
    *parts, rows_ref = refs
    count = len(parts)
    size = rows_ref.shape[0] // count
    me = position(hop)
    for k, part in enumerate(parts):
        at = pl.multiple_of(lax.rem(me + (count - k), count) * size, size)
        rows_ref[pl.ds(at, size), :] = part[...]


def send_ahead(block, hop, k):
    size = lax.axis_size("seq")
    count = size // hop
    route = [(i, ((i // hop + k) % count) * hop + i % hop) for i in range(size)]
    return lax.ppermute(block, "seq", route)


def mirrored(block, dp_bits, seq_bits):
    n_dp, n_seq = lax.axis_size("dp"), lax.axis_size("seq")
    route = [
        (i * n_seq + j, (i ^ dp_bits) * n_seq + (j ^ seq_bits))
        for i in range(n_dp)
        for j in range(n_seq)
    ]
    return lax.ppermute(block, ("dp", "seq"), route)


def column_groups(hop):
    size = lax.axis_size("seq")
    return [list(range(first, size, hop)) for first in range(hop)]


def exchange_all(block, hop):
    count = lax.axis_size("seq") // hop
    cut = block.reshape(count, -1, block.shape[-1])
    swapped = lax.all_to_all(cut, "seq", 0, 0, axis_index_groups=column_groups(hop), tiled=True)
    return swapped.reshape(block.shape)


def to_columns(block, hop, after=()):
    count = lax.axis_size("seq") // hop
    rows, channels = block.shape
    if count != MAX_PERMUTES:
        return [exchange_all(block, hop)]
    pieces = call(
        functools.partial(cut_kernel, hop), [((rows // count, channels), BF16)] * count, [], [block], mib=2
    )
    if after:
        pieces, _ = lax.optimization_barrier((pieces, list(after)))
    return forward_pieces(pieces, hop)


def forward_pieces(pieces, hop):
    sent = {k: mirrored(pieces[k], 0, k * hop) for k in ORDER[: len(pieces) - 1]}
    return [pieces[0]] + [sent[k] for k in sorted(sent)]


def reduce_weights(keep, send, grads, hop, scale):
    n_blocks, _, rows, lanes = keep.shape
    width = lanes // 4
    count = lax.axis_size("seq") // hop
    half = (n_blocks, rows // 2, lanes)
    fourth = (n_blocks, rows // 4, lanes)
    received = mirrored(send, 1, 0)
    back = {}


    if count == MAX_PERMUTES:
        back[0] = grads[0]
        for k in range(1, count):
            back[k] = send_ahead(grads[k], hop, k)
    pieces = call(split_kernel, [(half, F32)] + [(half, BF16)] * 3, [], [keep, received])
    arrived = [pieces[0]] + [mirrored(pieces[k], 2 * (k // 2), k % 2) for k in range(1, 4)]
    if count == MAX_PERMUTES:
        keep, send = call(
            functools.partial(halve_kernel, hop), [(fourth, F32), (fourth, BF16)], [(half, F32)], arrived,
            [back[k] for k in NEED[0]],
        )
        (pair,) = call(sum_kernel, [(fourth, BF16)], [], [keep, mirrored(send, 0, hop)], [back[k] for k in NEED[1]])
        (own,) = call(sum_kernel, [(fourth, BF16)], [], [pair, mirrored(pair, 0, 2 * hop)], [back[k] for k in NEED[2]])
        parts = [own] + [mirrored(own, 0, hop * (k // 2) + k % 2) for k in range(1, 4)]
        back = [back[k] for k in range(count)]
    else:
        (plane,) = call(sum_kernel, [(half, F32)], [], arrived)
        own = lax.psum(plane, "seq", axis_index_groups=column_groups(hop)).astype(BF16)
        parts = [own, mirrored(own, 0, 1)]
        back = [exchange_all(grads[0], hop)]
    outs = call(
        functools.partial(finish_kernel, scale, hop, n_blocks),
        [((3, rows, width), F32), ((width, rows), F32)] * n_blocks,
        [((n_blocks, rows, lanes), F32)],
        parts,
    )
    return back, [outs[2 * i : 2 * i + 2] for i in range(n_blocks)]


def shards(
    inputs,
    cotangent,
    first_dilated_kernel,
    first_pointwise_weight,
    second_dilated_kernel,
    second_pointwise_weight,
):
    samples, rows, channels = inputs.shape
    width = first_pointwise_weight.shape[0]
    hop = DILATION_ONE // rows
    size = rows // (lax.axis_size("seq") // hop)
    shifts = (size, size * (DILATION_TWO // DILATION_ONE))
    total_rows = samples * lax.axis_size("dp") * rows * lax.axis_size("seq")
    scale = 1.0 / math.sqrt(total_rows)
    k1t = jnp.swapaxes(first_dilated_kernel, 1, 2)
    k2t = jnp.swapaxes(second_dilated_kernel, 1, 2)
    p1, p2 = first_pointwise_weight, second_pointwise_weight

    x_parts = to_columns(inputs.reshape(rows, channels), hop)
    g_parts = to_columns(cotangent.reshape(rows, channels), hop, [x_parts[k] for k in GATE if k < len(x_parts)])
    n_parts = len(x_parts)
    whole = ((rows, channels), BF16)
    pads = [((rows + 2 * shift, width), BF16) for shift in shifts]
    state = [((channels, rows), BF16), ((width, rows), BF16), ((rows, channels), F32), ((rows, width), F32)]
    act1_t, mid1_t, s_x, s_p1, act2_t, mid2_t, s_h, s_p2 = call(
        functools.partial(forward_kernel, shifts, hop, n_parts),
        state * 2,
        [
            whole,
            ((rows + 2 * shifts[0], channels), BF16),
            ((rows + 2 * shifts[1], channels), BF16),
            ((TILE, channels), BF16),
            ((TILE, width), F32),
        ],
        list(x_parts) + [k1t, p1, k2t],
        mib=16,
    )
    quarters = ((2, 2, channels // 4, 4 * width), BF16)
    *x_grads, keep, send = call(
        functools.partial(chain_kernel, shifts, hop, n_parts),
        [(x_parts[0].shape, BF16)] * n_parts + [quarters, quarters],
        [whole, pads[0], whole, pads[1], ((channels, 4 * width), F32), whole],
        list(g_parts) + [s_p1, s_h, s_p2, k2t, p1, p2, act1_t, mid1_t, act2_t, mid2_t, s_x, k1t],
        mib=16,
    )
    back, ((conv2, point2), (conv1, point1)) = reduce_weights(keep, send, x_grads, hop, scale)
    if n_parts == 1:
        (input_grad,) = back
    else:
        (input_grad,) = call(functools.partial(collect_kernel, hop), [whole], [], back)
    return input_grad.reshape(inputs.shape), conv1, point1, conv2, point2


def solution(mesh):
    return jax.shard_map(
        shards,
        mesh=mesh,
        in_specs=(P("dp", "seq", None), P("dp", "seq", None), P(), P(), P(), P()),
        out_specs=(
            P("dp", "seq", None),
            P(None, "dp", None),
            P(None, "dp"),
            P(None, "dp", None),
            P(None, "dp"),
        ),
        check_vma=False,
    )
```

```python
import functools
import math

import jax
import jax.numpy as jnp
from jax import lax
from jax.experimental import pallas as pl
from jax.experimental.pallas import tpu as pltpu
from jax.sharding import PartitionSpec as P

DILATION_ONE = 2048
DILATION_TWO = 4096
TILE = 256
WIDE_TILE = 512
CHUNK = 32
MAX_PERMUTES = 4
NEED = ((3,), (1,), (2,))
ORDER = (2, 3, 1)
GATE = (3,)
BF16 = jnp.bfloat16
F32 = jnp.float32
VMEM = pl.BlockSpec(memory_space=pltpu.VMEM)
ANY = pl.BlockSpec(memory_space=pl.ANY)


def gelu_parts(values):
    coeff = math.sqrt(2.0 / math.pi)
    square = values * values
    tanh_val = jnp.tanh(values * (coeff + (coeff * 0.044715) * square))
    half = 0.5 + 0.5 * tanh_val
    slope = half + half * (1.0 - tanh_val) * (values * (coeff + (3.0 * coeff * 0.044715) * square))
    return values * half, slope


def dot(left, right):
    return jnp.dot(left, right, preferred_element_type=F32)


def dot_nt(left, right):
    return lax.dot_general(left, right, (((1,), (1,)), ((), ())), preferred_element_type=F32)


def position(hop):
    return lax.axis_index("seq") // hop


def call(kernel, out_shapes, scratch, args, after=(), mib=8):
    n_args, n_after = len(args), len(after)

    def body(*refs):
        kernel(*refs[:n_args], *refs[n_args + n_after :])

    return pl.pallas_call(
        body,
        out_shape=[jax.ShapeDtypeStruct(s, d) for s, d in out_shapes],
        in_specs=[VMEM] * n_args + [ANY] * n_after,
        out_specs=[VMEM] * len(out_shapes),
        scratch_shapes=[pltpu.VMEM(s, d) for s, d in scratch],
        compiler_params=pltpu.CompilerParams(vmem_limit_bytes=mib << 20),
    )(*args, *after)


def cut_kernel(hop, block, *pieces):
    count = len(pieces)
    size = pieces[0].shape[0]
    me = position(hop)
    for k, piece in enumerate(pieces):
        at = pl.multiple_of((me ^ k) * size, size)
        piece[...] = block[pl.ds(at, size), :]


def place(parts, rows_ref, hop):
    if len(parts) == 1:
        rows_ref[...] = parts[0][...]
        return
    count = len(parts)
    size = rows_ref.shape[0] // count
    me = position(hop)
    for k, part in enumerate(parts):
        at = pl.multiple_of((me ^ k) * size, size)
        rows_ref[pl.ds(at, size), :] = part[...]


def hand_out(rows_ref, parts, hop):
    if len(parts) == 1:
        parts[0][...] = rows_ref[...]
        return
    count = len(parts)
    size = rows_ref.shape[0] // count
    me = position(hop)
    for k, part in enumerate(parts):
        at = pl.multiple_of(lax.rem(me + k, count) * size, size)
        part[...] = rows_ref[pl.ds(at, size), :]


def tap_sum(padded_ref, shift, start, tile, weight_of, mm):
    total = mm(padded_ref[pl.ds(start + shift, tile), :], weight_of(1))
    rows = padded_ref.shape[0] - 2 * shift
    if start + tile > shift:
        total = total + mm(padded_ref[pl.ds(start, tile), :], weight_of(0))
    if start < rows - shift:
        total = total + mm(padded_ref[pl.ds(start + 2 * shift, tile), :], weight_of(2))
    return total


def clear_edges(padded_ref, shift):
    if shift % TILE == 0:
        return
    rows = padded_ref.shape[0]
    zeros = jnp.zeros((shift, padded_ref.shape[1]), padded_ref.dtype)
    padded_ref[pl.ds(0, shift), :] = zeros
    padded_ref[pl.ds(rows - shift, shift), :] = zeros


def forward_kernel(shifts, hop, count, *refs):
    parts = refs[:count]
    weights = refs[count : count + 3]
    outs = refs[count + 3 : count + 11]
    scratch = refs[count + 11 :]
    place(parts, scratch[0], hop)
    forward_rows(shifts, weights, outs, scratch)


def forward_rows(shifts, weights, outs, scratch):
    k1t, p1, k2t = weights
    act1_t, mid1_t, s_x, s_p1, act2_t, mid2_t, s_h, s_p2 = outs
    x_rows, pad1, pad2, wide, narrow = scratch
    rows = x_rows.shape[0]

    def activate(source, source_start, pad, shift, start, slope_ref):
        def step(i, carry):
            at = pl.multiple_of(i * CHUNK, CHUNK)
            value, slope = gelu_parts(source[pl.ds(source_start + at, CHUNK), :].astype(F32))
            pad[pl.ds(start + shift + at, CHUNK), :] = value.astype(BF16)
            slope_ref[pl.ds(start + at, CHUNK), :] = slope
            return carry

        lax.fori_loop(0, TILE // CHUNK, step, 0, unroll=2)

    def narrow_gelu(start, slope_ref):
        def step(i, carry):
            at = pl.multiple_of(i * CHUNK, CHUNK)
            value, slope = gelu_parts(narrow[pl.ds(at, CHUNK), :])
            narrow[pl.ds(at, CHUNK), :] = value
            slope_ref[pl.ds(start + at, CHUNK), :] = slope
            return carry

        lax.fori_loop(0, TILE // CHUNK, step, 0, unroll=2)

    clear_edges(pad1, shifts[0])
    clear_edges(pad2, shifts[1])
    for start in range(0, rows, TILE):
        activate(x_rows, start, pad1, shifts[0], start, s_x)
        act1_t[:, pl.ds(start, TILE)] = pad1[pl.ds(start + shifts[0], TILE), :].T
    for start in range(0, rows, TILE):
        narrow[...] = tap_sum(pad1, shifts[0], start, TILE, lambda k: k1t[k], dot_nt)
        narrow_gelu(start, s_p1)
        mid = narrow[...].astype(BF16)
        mid1_t[:, pl.ds(start, TILE)] = mid.T
        wide[...] = (x_rows[pl.ds(start, TILE), :].astype(F32) + dot(mid, p1[...])).astype(BF16)
        activate(wide, 0, pad2, shifts[1], start, s_h)
        act2_t[:, pl.ds(start, TILE)] = pad2[pl.ds(start + shifts[1], TILE), :].T
    for start in range(0, rows, TILE):
        narrow[...] = tap_sum(pad2, shifts[1], start, TILE, lambda k: k2t[k], dot_nt)
        narrow_gelu(start, s_p2)
        mid2_t[:, pl.ds(start, TILE)] = narrow[...].astype(BF16).T


def chain_kernel(shifts, hop, n_in, *refs):
    parts = refs[:n_in]
    s_p1, s_h, s_p2, k2t, p1, p2, act1_t, mid1_t, act2_t, mid2_t = refs[n_in : n_in + 10]
    s_x, k1t = refs[n_in + 10 : n_in + 12]
    outs = refs[n_in + 12 : -8]
    keep, send, g1_rows, pad1, g2_rows, pad2, grads, x_rows = refs[-8:]
    place(parts, g2_rows, hop)
    middle_rows(shifts[1], g2_rows, pad2, s_p2, p2)
    outer_rows(shifts[1], g2_rows, pad2, s_h, k2t, g1_rows)
    middle_rows(shifts[0], g1_rows, pad1, s_p1, p1)
    weights_kernel(
        shifts[::-1], act2_t, mid2_t, pad2, g2_rows, act1_t, mid1_t, pad1, g1_rows, keep, send, grads
    )
    outer_rows(shifts[0], g1_rows, pad1, s_x, k1t, x_rows)
    hand_out(x_rows, outs, hop)


def middle_rows(shift, g_rows, pad, s_pre, point):
    clear_edges(pad, shift)
    for start in range(0, g_rows.shape[0], WIDE_TILE):
        mid_grad = dot_nt(g_rows[pl.ds(start, WIDE_TILE), :], point[...])
        pad[pl.ds(start + shift, WIDE_TILE), :] = (mid_grad * s_pre[pl.ds(start, WIDE_TILE), :]).astype(BF16)


def outer_rows(shift, g_rows, pad, s_state, kt, x_rows):
    for start in range(0, g_rows.shape[0], TILE):
        act_grad = tap_sum(pad, shift, start, TILE, lambda k: kt[2 - k], dot)
        x_rows[pl.ds(start, TILE), :] = (
            g_rows[pl.ds(start, TILE), :].astype(F32) + act_grad * s_state[pl.ds(start, TILE), :]
        ).astype(BF16)


def weights_kernel(shifts, *refs):
    keep, send, grads = refs[-3:]
    size = keep.shape[2]
    core = lax.rem(lax.axis_index("dp"), 2)
    for i, shift in enumerate(shifts):
        act_t, mid_t, pad, g_rows = refs[4 * i : 4 * i + 4]
        rows = g_rows.shape[0]
        act = act_t[...]
        near = rows - shift if shift % 128 == 0 else rows
        grads[...] = jnp.concatenate(
            [
                dot(act[:, :near], pad[pl.ds(2 * shift, near), :]),
                dot(act, pad[pl.ds(shift, rows), :]),
                dot(act[:, rows - near :], pad[pl.ds(rows - near, near), :]),
                dot(mid_t[...], g_rows[...]).T,
            ],
            axis=1,
        )
        for x_to in range(2):
            for target, parity in ((keep, core), (send, 1 - core)):
                rows_at = pl.multiple_of((2 * x_to + parity) * size, size)
                target[i, x_to] = grads[pl.ds(rows_at, size), :].astype(target.dtype)


def split_kernel(keep, received, *pieces):
    x_at = lax.axis_index("dp") // 2
    y_at = lax.rem(lax.axis_index("seq"), 2)
    size = pieces[0].shape[1]
    for k, piece in enumerate(pieces):
        x_to = lax.rem(x_at + k // 2, 2)
        rows = pl.ds(pl.multiple_of(lax.rem(y_at + k, 2) * size, size), size)
        for i in range(keep.shape[0]):
            total = keep[i, x_to, rows, :].astype(F32) + received[i, x_to, rows, :].astype(F32)
            piece[i] = total.astype(piece.dtype)


def sum_of(refs):
    total = refs[0][...].astype(F32)
    for ref in refs[1:]:
        total = total + ref[...].astype(F32)
    return total


def sum_kernel(*refs):
    refs[-1][...] = sum_of(refs[:-1]).astype(refs[-1].dtype)


def halve_kernel(hop, *refs):
    *parts, keep, send, total = refs
    total[...] = sum_of(parts)
    size = keep.shape[1]
    mine = lax.rem(position(hop), 2)
    for target, half in ((keep, mine), (send, 1 - mine)):
        target[...] = total[:, pl.ds(pl.multiple_of(half * size, size), size), :].astype(target.dtype)


def finish_kernel(scale, hop, n_blocks, *refs):
    parts, outs, rows = refs[: -2 * n_blocks - 1], refs[-2 * n_blocks - 1 : -1], refs[-1]
    z_at = lax.rem(position(hop), 2)
    y_at = lax.rem(lax.axis_index("seq"), 2)
    size = parts[0].shape[1]
    per_y = rows.shape[1] // 2
    for k, part in enumerate(parts):
        at = lax.rem(y_at + k, 2) * per_y
        if len(parts) > 2:
            at = at + lax.rem(z_at + k // 2, 2) * size
        rows[:, pl.ds(pl.multiple_of(at, size), size), :] = part[...].astype(F32) * scale
    for i in range(n_blocks):
        conv, point = outs[2 * i : 2 * i + 2]
        width = conv.shape[2]
        whole = rows[i]
        for k in range(3):
            conv[k] = whole[:, k * width : (k + 1) * width]
        point[...] = whole[:, 3 * width :].T


def collect_kernel(hop, *refs):
    *parts, rows_ref = refs
    count = len(parts)
    size = rows_ref.shape[0] // count
    me = position(hop)
    for k, part in enumerate(parts):
        at = pl.multiple_of(lax.rem(me + (count - k), count) * size, size)
        rows_ref[pl.ds(at, size), :] = part[...]


def send_ahead(block, hop, k):
    size = lax.axis_size("seq")
    count = size // hop
    route = [(i, ((i // hop + k) % count) * hop + i % hop) for i in range(size)]
    return lax.ppermute(block, "seq", route)


def mirrored(block, dp_bits, seq_bits):
    n_dp, n_seq = lax.axis_size("dp"), lax.axis_size("seq")
    route = [
        (i * n_seq + j, (i ^ dp_bits) * n_seq + (j ^ seq_bits))
        for i in range(n_dp)
        for j in range(n_seq)
    ]
    return lax.ppermute(block, ("dp", "seq"), route)


def column_groups(hop):
    size = lax.axis_size("seq")
    return [list(range(first, size, hop)) for first in range(hop)]


def exchange_all(block, hop):
    count = lax.axis_size("seq") // hop
    cut = block.reshape(count, -1, block.shape[-1])
    swapped = lax.all_to_all(cut, "seq", 0, 0, axis_index_groups=column_groups(hop), tiled=True)
    return swapped.reshape(block.shape)


def to_columns(block, hop, after=()):
    count = lax.axis_size("seq") // hop
    rows, channels = block.shape
    if count != MAX_PERMUTES:
        return [exchange_all(block, hop)]
    pieces = call(
        functools.partial(cut_kernel, hop), [((rows // count, channels), BF16)] * count, [], [block], mib=2
    )
    if after:
        pieces, _ = lax.optimization_barrier((pieces, list(after)))
    return forward_pieces(pieces, hop)


def forward_pieces(pieces, hop):
    sent = {k: mirrored(pieces[k], 0, k * hop) for k in ORDER[: len(pieces) - 1]}
    return [pieces[0]] + [sent[k] for k in sorted(sent)]


def reduce_weights(keep, send, grads, hop, scale):
    n_blocks, _, rows, lanes = keep.shape
    width = lanes // 4
    count = lax.axis_size("seq") // hop
    half = (n_blocks, rows // 2, lanes)
    fourth = (n_blocks, rows // 4, lanes)
    received = mirrored(send, 1, 0)
    back = {}


    if count == MAX_PERMUTES:
        back[0] = grads[0]
        for k in range(1, count):
            back[k] = send_ahead(grads[k], hop, k)
    pieces = call(split_kernel, [(half, F32)] + [(half, BF16)] * 3, [], [keep, received])
    arrived = [pieces[0]] + [mirrored(pieces[k], 2 * (k // 2), k % 2) for k in range(1, 4)]
    if count == MAX_PERMUTES:
        keep, send = call(
            functools.partial(halve_kernel, hop), [(fourth, F32), (fourth, BF16)], [(half, F32)], arrived,
            [back[k] for k in NEED[0]],
        )
        (pair,) = call(sum_kernel, [(fourth, BF16)], [], [keep, mirrored(send, 0, hop)], [back[k] for k in NEED[1]])
        (own,) = call(sum_kernel, [(fourth, BF16)], [], [pair, mirrored(pair, 0, 2 * hop)], [back[k] for k in NEED[2]])
        parts = [own] + [mirrored(own, 0, hop * (k // 2) + k % 2) for k in range(1, 4)]
        back = [back[k] for k in range(count)]
    else:
        (plane,) = call(sum_kernel, [(half, F32)], [], arrived)
        own = lax.psum(plane, "seq", axis_index_groups=column_groups(hop)).astype(BF16)
        parts = [own, mirrored(own, 0, 1)]
        back = [exchange_all(grads[0], hop)]
    outs = call(
        functools.partial(finish_kernel, scale, hop, n_blocks),
        [((3, rows, width), F32), ((width, rows), F32)] * n_blocks,
        [((n_blocks, rows, lanes), F32)],
        parts,
    )
    return back, [outs[2 * i : 2 * i + 2] for i in range(n_blocks)]


def shards(
    inputs,
    cotangent,
    first_dilated_kernel,
    first_pointwise_weight,
    second_dilated_kernel,
    second_pointwise_weight,
):
    samples, rows, channels = inputs.shape
    width = first_pointwise_weight.shape[0]
    hop = DILATION_ONE // rows
    size = rows // (lax.axis_size("seq") // hop)
    shifts = (size, size * (DILATION_TWO // DILATION_ONE))
    total_rows = samples * lax.axis_size("dp") * rows * lax.axis_size("seq")
    scale = 1.0 / math.sqrt(total_rows)
    k1t = jnp.swapaxes(first_dilated_kernel, 1, 2)
    k2t = jnp.swapaxes(second_dilated_kernel, 1, 2)
    p1, p2 = first_pointwise_weight, second_pointwise_weight

    x_parts = to_columns(inputs.reshape(rows, channels), hop)
    g_parts = to_columns(cotangent.reshape(rows, channels), hop, [x_parts[k] for k in GATE if k < len(x_parts)])
    n_parts = len(x_parts)
    whole = ((rows, channels), BF16)
    pads = [((rows + 2 * shift, width), BF16) for shift in shifts]
    state = [((channels, rows), BF16), ((width, rows), BF16), ((rows, channels), F32), ((rows, width), F32)]
    act1_t, mid1_t, s_x, s_p1, act2_t, mid2_t, s_h, s_p2 = call(
        functools.partial(forward_kernel, shifts, hop, n_parts),
        state * 2,
        [
            whole,
            ((rows + 2 * shifts[0], channels), BF16),
            ((rows + 2 * shifts[1], channels), BF16),
            ((TILE, channels), BF16),
            ((TILE, width), F32),
        ],
        list(x_parts) + [k1t, p1, k2t],
        mib=16,
    )
    quarters = ((2, 2, channels // 4, 4 * width), BF16)
    *x_grads, keep, send = call(
        functools.partial(chain_kernel, shifts, hop, n_parts),
        [(x_parts[0].shape, BF16)] * n_parts + [quarters, quarters],
        [whole, pads[0], whole, pads[1], ((channels, 4 * width), F32), whole],
        list(g_parts) + [s_p1, s_h, s_p2, k2t, p1, p2, act1_t, mid1_t, act2_t, mid2_t, s_x, k1t],
        mib=16,
    )
    back, ((conv2, point2), (conv1, point1)) = reduce_weights(keep, send, x_grads, hop, scale)
    if n_parts == 1:
        (input_grad,) = back
    else:
        (input_grad,) = call(functools.partial(collect_kernel, hop), [whole], [], back)
    return input_grad.reshape(inputs.shape), conv1, point1, conv2, point2


def solution(mesh):
    return jax.shard_map(
        shards,
        mesh=mesh,
        in_specs=(P("dp", "seq", None), P("dp", "seq", None), P(), P(), P(), P()),
        out_specs=(
            P("dp", "seq", None),
            P(None, "dp", None),
            P(None, "dp"),
            P(None, "dp", None),
            P(None, "dp"),
        ),
        check_vma=False,
    )
```

```python
import functools
import math

import jax
import jax.numpy as jnp
from jax import lax
from jax.experimental import pallas as pl
from jax.experimental.pallas import tpu as pltpu
from jax.sharding import PartitionSpec as P

DILATION_ONE = 2048
DILATION_TWO = 4096
TILE = 256
WIDE_TILE = 512
CHUNK = 32
MAX_PERMUTES = 4
NEED = ((3,), (), (1, 2))
ORDER = (2, 3, 1)
GATE = (3,)
BF16 = jnp.bfloat16
F32 = jnp.float32
VMEM = pl.BlockSpec(memory_space=pltpu.VMEM)
ANY = pl.BlockSpec(memory_space=pl.ANY)


def gelu_parts(values):
    coeff = math.sqrt(2.0 / math.pi)
    square = values * values
    tanh_val = jnp.tanh(values * (coeff + (coeff * 0.044715) * square))
    half = 0.5 + 0.5 * tanh_val
    slope = half + half * (1.0 - tanh_val) * (values * (coeff + (3.0 * coeff * 0.044715) * square))
    return values * half, slope


def dot(left, right):
    return jnp.dot(left, right, preferred_element_type=F32)


def dot_nt(left, right):
    return lax.dot_general(left, right, (((1,), (1,)), ((), ())), preferred_element_type=F32)


def position(hop):
    return lax.axis_index("seq") // hop


def call(kernel, out_shapes, scratch, args, after=(), mib=8):
    n_args, n_after = len(args), len(after)

    def body(*refs):
        kernel(*refs[:n_args], *refs[n_args + n_after :])

    return pl.pallas_call(
        body,
        out_shape=[jax.ShapeDtypeStruct(s, d) for s, d in out_shapes],
        in_specs=[VMEM] * n_args + [ANY] * n_after,
        out_specs=[VMEM] * len(out_shapes),
        scratch_shapes=[pltpu.VMEM(s, d) for s, d in scratch],
        compiler_params=pltpu.CompilerParams(vmem_limit_bytes=mib << 20),
    )(*args, *after)


def cut_kernel(hop, block, *pieces):
    count = len(pieces)
    size = pieces[0].shape[0]
    me = position(hop)
    for k, piece in enumerate(pieces):
        at = pl.multiple_of((me ^ k) * size, size)
        piece[...] = block[pl.ds(at, size), :]


def place(parts, rows_ref, hop):
    if len(parts) == 1:
        rows_ref[...] = parts[0][...]
        return
    count = len(parts)
    size = rows_ref.shape[0] // count
    me = position(hop)
    for k, part in enumerate(parts):
        at = pl.multiple_of((me ^ k) * size, size)
        rows_ref[pl.ds(at, size), :] = part[...]


def hand_out(rows_ref, parts, hop):
    if len(parts) == 1:
        parts[0][...] = rows_ref[...]
        return
    count = len(parts)
    size = rows_ref.shape[0] // count
    me = position(hop)
    for k, part in enumerate(parts):
        at = pl.multiple_of(lax.rem(me + k, count) * size, size)
        part[...] = rows_ref[pl.ds(at, size), :]


def tap_sum(padded_ref, shift, start, tile, weight_of, mm):
    total = mm(padded_ref[pl.ds(start + shift, tile), :], weight_of(1))
    rows = padded_ref.shape[0] - 2 * shift
    if start + tile > shift:
        total = total + mm(padded_ref[pl.ds(start, tile), :], weight_of(0))
    if start < rows - shift:
        total = total + mm(padded_ref[pl.ds(start + 2 * shift, tile), :], weight_of(2))
    return total


def clear_edges(padded_ref, shift):
    if shift % TILE == 0:
        return
    rows = padded_ref.shape[0]
    zeros = jnp.zeros((shift, padded_ref.shape[1]), padded_ref.dtype)
    padded_ref[pl.ds(0, shift), :] = zeros
    padded_ref[pl.ds(rows - shift, shift), :] = zeros


def forward_kernel(shifts, hop, count, *refs):
    parts = refs[:count]
    weights = refs[count : count + 3]
    outs = refs[count + 3 : count + 11]
    scratch = refs[count + 11 :]
    place(parts, scratch[0], hop)
    forward_rows(shifts, weights, outs, scratch)


def forward_rows(shifts, weights, outs, scratch):
    k1t, p1, k2t = weights
    act1_t, mid1_t, s_x, s_p1, act2_t, mid2_t, s_h, s_p2 = outs
    x_rows, pad1, pad2, wide, narrow = scratch
    rows = x_rows.shape[0]

    def activate(source, source_start, pad, shift, start, slope_ref):
        def step(i, carry):
            at = pl.multiple_of(i * CHUNK, CHUNK)
            value, slope = gelu_parts(source[pl.ds(source_start + at, CHUNK), :].astype(F32))
            pad[pl.ds(start + shift + at, CHUNK), :] = value.astype(BF16)
            slope_ref[pl.ds(start + at, CHUNK), :] = slope
            return carry

        lax.fori_loop(0, TILE // CHUNK, step, 0, unroll=2)

    def narrow_gelu(start, slope_ref):
        def step(i, carry):
            at = pl.multiple_of(i * CHUNK, CHUNK)
            value, slope = gelu_parts(narrow[pl.ds(at, CHUNK), :])
            narrow[pl.ds(at, CHUNK), :] = value
            slope_ref[pl.ds(start + at, CHUNK), :] = slope
            return carry

        lax.fori_loop(0, TILE // CHUNK, step, 0, unroll=2)

    clear_edges(pad1, shifts[0])
    clear_edges(pad2, shifts[1])
    for start in range(0, rows, TILE):
        activate(x_rows, start, pad1, shifts[0], start, s_x)
        act1_t[:, pl.ds(start, TILE)] = pad1[pl.ds(start + shifts[0], TILE), :].T
    for start in range(0, rows, TILE):
        narrow[...] = tap_sum(pad1, shifts[0], start, TILE, lambda k: k1t[k], dot_nt)
        narrow_gelu(start, s_p1)
        mid = narrow[...].astype(BF16)
        mid1_t[:, pl.ds(start, TILE)] = mid.T
        wide[...] = (x_rows[pl.ds(start, TILE), :].astype(F32) + dot(mid, p1[...])).astype(BF16)
        activate(wide, 0, pad2, shifts[1], start, s_h)
        act2_t[:, pl.ds(start, TILE)] = pad2[pl.ds(start + shifts[1], TILE), :].T
    for start in range(0, rows, TILE):
        narrow[...] = tap_sum(pad2, shifts[1], start, TILE, lambda k: k2t[k], dot_nt)
        narrow_gelu(start, s_p2)
        mid2_t[:, pl.ds(start, TILE)] = narrow[...].astype(BF16).T


def chain_kernel(shifts, hop, n_in, *refs):
    parts = refs[:n_in]
    s_p1, s_h, s_p2, k2t, p1, p2, act1_t, mid1_t, act2_t, mid2_t = refs[n_in : n_in + 10]
    s_x, k1t = refs[n_in + 10 : n_in + 12]
    outs = refs[n_in + 12 : -8]
    keep, send, g1_rows, pad1, g2_rows, pad2, grads, x_rows = refs[-8:]
    place(parts, g2_rows, hop)
    middle_rows(shifts[1], g2_rows, pad2, s_p2, p2)
    outer_rows(shifts[1], g2_rows, pad2, s_h, k2t, g1_rows)
    middle_rows(shifts[0], g1_rows, pad1, s_p1, p1)
    weights_kernel(
        shifts[::-1], act2_t, mid2_t, pad2, g2_rows, act1_t, mid1_t, pad1, g1_rows, keep, send, grads
    )
    outer_rows(shifts[0], g1_rows, pad1, s_x, k1t, x_rows)
    hand_out(x_rows, outs, hop)


def middle_rows(shift, g_rows, pad, s_pre, point):
    clear_edges(pad, shift)
    for start in range(0, g_rows.shape[0], WIDE_TILE):
        mid_grad = dot_nt(g_rows[pl.ds(start, WIDE_TILE), :], point[...])
        pad[pl.ds(start + shift, WIDE_TILE), :] = (mid_grad * s_pre[pl.ds(start, WIDE_TILE), :]).astype(BF16)


def outer_rows(shift, g_rows, pad, s_state, kt, x_rows):
    for start in range(0, g_rows.shape[0], TILE):
        act_grad = tap_sum(pad, shift, start, TILE, lambda k: kt[2 - k], dot)
        x_rows[pl.ds(start, TILE), :] = (
            g_rows[pl.ds(start, TILE), :].astype(F32) + act_grad * s_state[pl.ds(start, TILE), :]
        ).astype(BF16)


def weights_kernel(shifts, *refs):
    keep, send, grads = refs[-3:]
    size = keep.shape[2]
    core = lax.rem(lax.axis_index("dp"), 2)
    for i, shift in enumerate(shifts):
        act_t, mid_t, pad, g_rows = refs[4 * i : 4 * i + 4]
        rows = g_rows.shape[0]
        act = act_t[...]
        near = rows - shift if shift % 128 == 0 else rows
        grads[...] = jnp.concatenate(
            [
                dot(act[:, :near], pad[pl.ds(2 * shift, near), :]),
                dot(act, pad[pl.ds(shift, rows), :]),
                dot(act[:, rows - near :], pad[pl.ds(rows - near, near), :]),
                dot(mid_t[...], g_rows[...]).T,
            ],
            axis=1,
        )
        for x_to in range(2):
            for target, parity in ((keep, core), (send, 1 - core)):
                rows_at = pl.multiple_of((2 * x_to + parity) * size, size)
                target[i, x_to] = grads[pl.ds(rows_at, size), :].astype(target.dtype)


def split_kernel(keep, received, *pieces):
    x_at = lax.axis_index("dp") // 2
    y_at = lax.rem(lax.axis_index("seq"), 2)
    size = pieces[0].shape[1]
    for k, piece in enumerate(pieces):
        x_to = lax.rem(x_at + k // 2, 2)
        rows = pl.ds(pl.multiple_of(lax.rem(y_at + k, 2) * size, size), size)
        for i in range(keep.shape[0]):
            total = keep[i, x_to, rows, :].astype(F32) + received[i, x_to, rows, :].astype(F32)
            piece[i] = total.astype(piece.dtype)


def sum_of(refs):
    total = refs[0][...].astype(F32)
    for ref in refs[1:]:
        total = total + ref[...].astype(F32)
    return total


def sum_kernel(*refs):
    refs[-1][...] = sum_of(refs[:-1]).astype(refs[-1].dtype)


def halve_kernel(hop, *refs):
    *parts, keep, send, total = refs
    total[...] = sum_of(parts)
    size = keep.shape[1]
    mine = lax.rem(position(hop), 2)
    for target, half in ((keep, mine), (send, 1 - mine)):
        target[...] = total[:, pl.ds(pl.multiple_of(half * size, size), size), :].astype(target.dtype)


def finish_kernel(scale, hop, n_blocks, *refs):
    parts, outs, rows = refs[: -2 * n_blocks - 1], refs[-2 * n_blocks - 1 : -1], refs[-1]
    z_at = lax.rem(position(hop), 2)
    y_at = lax.rem(lax.axis_index("seq"), 2)
    size = parts[0].shape[1]
    per_y = rows.shape[1] // 2
    for k, part in enumerate(parts):
        at = lax.rem(y_at + k, 2) * per_y
        if len(parts) > 2:
            at = at + lax.rem(z_at + k // 2, 2) * size
        rows[:, pl.ds(pl.multiple_of(at, size), size), :] = part[...].astype(F32) * scale
    for i in range(n_blocks):
        conv, point = outs[2 * i : 2 * i + 2]
        width = conv.shape[2]
        whole = rows[i]
        for k in range(3):
            conv[k] = whole[:, k * width : (k + 1) * width]
        point[...] = whole[:, 3 * width :].T


def collect_kernel(hop, *refs):
    *parts, rows_ref = refs
    count = len(parts)
    size = rows_ref.shape[0] // count
    me = position(hop)
    for k, part in enumerate(parts):
        at = pl.multiple_of(lax.rem(me + (count - k), count) * size, size)
        rows_ref[pl.ds(at, size), :] = part[...]


def send_ahead(block, hop, k):
    size = lax.axis_size("seq")
    count = size // hop
    route = [(i, ((i // hop + k) % count) * hop + i % hop) for i in range(size)]
    return lax.ppermute(block, "seq", route)


def mirrored(block, dp_bits, seq_bits):
    n_dp, n_seq = lax.axis_size("dp"), lax.axis_size("seq")
    route = [
        (i * n_seq + j, (i ^ dp_bits) * n_seq + (j ^ seq_bits))
        for i in range(n_dp)
        for j in range(n_seq)
    ]
    return lax.ppermute(block, ("dp", "seq"), route)


def column_groups(hop):
    size = lax.axis_size("seq")
    return [list(range(first, size, hop)) for first in range(hop)]


def exchange_all(block, hop):
    count = lax.axis_size("seq") // hop
    cut = block.reshape(count, -1, block.shape[-1])
    swapped = lax.all_to_all(cut, "seq", 0, 0, axis_index_groups=column_groups(hop), tiled=True)
    return swapped.reshape(block.shape)


def to_columns(block, hop, after=()):
    count = lax.axis_size("seq") // hop
    rows, channels = block.shape
    if count != MAX_PERMUTES:
        return [exchange_all(block, hop)]
    pieces = call(
        functools.partial(cut_kernel, hop), [((rows // count, channels), BF16)] * count, [], [block], mib=2
    )
    if after:
        pieces, _ = lax.optimization_barrier((pieces, list(after)))
    return forward_pieces(pieces, hop)


def forward_pieces(pieces, hop):
    sent = {k: mirrored(pieces[k], 0, k * hop) for k in ORDER[: len(pieces) - 1]}
    return [pieces[0]] + [sent[k] for k in sorted(sent)]


def reduce_weights(keep, send, grads, hop, scale):
    n_blocks, _, rows, lanes = keep.shape
    width = lanes // 4
    count = lax.axis_size("seq") // hop
    half = (n_blocks, rows // 2, lanes)
    fourth = (n_blocks, rows // 4, lanes)
    received = mirrored(send, 1, 0)
    back = {}


    if count == MAX_PERMUTES:
        back[0] = grads[0]
        for k in range(1, count):
            back[k] = send_ahead(grads[k], hop, k)
    pieces = call(split_kernel, [(half, F32)] + [(half, BF16)] * 3, [], [keep, received])
    arrived = [pieces[0]] + [mirrored(pieces[k], 2 * (k // 2), k % 2) for k in range(1, 4)]
    if count == MAX_PERMUTES:
        keep, send = call(
            functools.partial(halve_kernel, hop), [(fourth, F32), (fourth, BF16)], [(half, F32)], arrived,
            [back[k] for k in NEED[0]],
        )
        (pair,) = call(sum_kernel, [(fourth, BF16)], [], [keep, mirrored(send, 0, hop)], [back[k] for k in NEED[1]])
        (own,) = call(sum_kernel, [(fourth, BF16)], [], [pair, mirrored(pair, 0, 2 * hop)], [back[k] for k in NEED[2]])
        parts = [own] + [mirrored(own, 0, hop * (k // 2) + k % 2) for k in range(1, 4)]
        back = [back[k] for k in range(count)]
    else:
        (plane,) = call(sum_kernel, [(half, F32)], [], arrived)
        own = lax.psum(plane, "seq", axis_index_groups=column_groups(hop)).astype(BF16)
        parts = [own, mirrored(own, 0, 1)]
        back = [exchange_all(grads[0], hop)]
    outs = call(
        functools.partial(finish_kernel, scale, hop, n_blocks),
        [((3, rows, width), F32), ((width, rows), F32)] * n_blocks,
        [((n_blocks, rows, lanes), F32)],
        parts,
    )
    return back, [outs[2 * i : 2 * i + 2] for i in range(n_blocks)]


def shards(
    inputs,
    cotangent,
    first_dilated_kernel,
    first_pointwise_weight,
    second_dilated_kernel,
    second_pointwise_weight,
):
    samples, rows, channels = inputs.shape
    width = first_pointwise_weight.shape[0]
    hop = DILATION_ONE // rows
    size = rows // (lax.axis_size("seq") // hop)
    shifts = (size, size * (DILATION_TWO // DILATION_ONE))
    total_rows = samples * lax.axis_size("dp") * rows * lax.axis_size("seq")
    scale = 1.0 / math.sqrt(total_rows)
    k1t = jnp.swapaxes(first_dilated_kernel, 1, 2)
    k2t = jnp.swapaxes(second_dilated_kernel, 1, 2)
    p1, p2 = first_pointwise_weight, second_pointwise_weight

    x_parts = to_columns(inputs.reshape(rows, channels), hop)
    g_parts = to_columns(cotangent.reshape(rows, channels), hop, [x_parts[k] for k in GATE if k < len(x_parts)])
    n_parts = len(x_parts)
    whole = ((rows, channels), BF16)
    pads = [((rows + 2 * shift, width), BF16) for shift in shifts]
    state = [((channels, rows), BF16), ((width, rows), BF16), ((rows, channels), F32), ((rows, width), F32)]
    act1_t, mid1_t, s_x, s_p1, act2_t, mid2_t, s_h, s_p2 = call(
        functools.partial(forward_kernel, shifts, hop, n_parts),
        state * 2,
        [
            whole,
            ((rows + 2 * shifts[0], channels), BF16),
            ((rows + 2 * shifts[1], channels), BF16),
            ((TILE, channels), BF16),
            ((TILE, width), F32),
        ],
        list(x_parts) + [k1t, p1, k2t],
        mib=16,
    )
    quarters = ((2, 2, channels // 4, 4 * width), BF16)
    *x_grads, keep, send = call(
        functools.partial(chain_kernel, shifts, hop, n_parts),
        [(x_parts[0].shape, BF16)] * n_parts + [quarters, quarters],
        [whole, pads[0], whole, pads[1], ((channels, 4 * width), F32), whole],
        list(g_parts) + [s_p1, s_h, s_p2, k2t, p1, p2, act1_t, mid1_t, act2_t, mid2_t, s_x, k1t],
        mib=16,
    )
    back, ((conv2, point2), (conv1, point1)) = reduce_weights(keep, send, x_grads, hop, scale)
    if n_parts == 1:
        (input_grad,) = back
    else:
        (input_grad,) = call(functools.partial(collect_kernel, hop), [whole], [], back)
    return input_grad.reshape(inputs.shape), conv1, point1, conv2, point2


def solution(mesh):
    return jax.shard_map(
        shards,
        mesh=mesh,
        in_specs=(P("dp", "seq", None), P("dp", "seq", None), P(), P(), P(), P()),
        out_specs=(
            P("dp", "seq", None),
            P(None, "dp", None),
            P(None, "dp"),
            P(None, "dp", None),
            P(None, "dp"),
        ),
        check_vma=False,
    )
```
